256 devices in a mesh: gx: 32 (over x, y, core), gy: 8 (over z).
Axes of the slice: x: 4, y: 4, z: 8, core: 2. Of those that a mesh axis runs over, the one named last changes fastest.
Arguments:
- leaf_maps: float32 [32, 8, 1024, 1024], P('gx', 'gy'), may hold values from -8 to 40, as said below
- edge_data: float32 [32, 8, 512, 1024], P('gx', 'gy'), may hold values from -6 to 6
Outputs:
- potential: float32 [32, 8, 1024, 1024], P('gx', 'gy')
- flux: float32 [32, 8, 1024, 1024], P('gx', 'gy')
The draws below stay inside these ranges and needn't reach their ends.
Inputs may be any that keep to these rules, and one draw needn't show every extreme that they name: `leaf_maps`: each leaf's map is exactly symmetric and positive definite.
All inputs are finite; a program needn't handle non-finite values.
Results may differ from the reference program's by a relative error of at most 0.0003.
Values sent between devices are 32-bit elements; how exact they have to be, the bound alone decides.
A program may use at most 128 MiB of HBM per device.

```python
import math
import jax
import jax.numpy as jnp
from jax import lax

EDGE = 256
RHS_COUNT = 1024
BOX_COLS = 32
BOX_ROWS = 8


def draw_leaf_maps(key, part):
    full_len = 4 * EDGE
    shared = jax.random.fold_in(key, 101)
    raw = jax.random.normal(jax.random.fold_in(shared, 1), (EDGE, EDGE), jnp.float32)
    basis, upper = jnp.linalg.qr(raw)
    signs = jnp.where(jnp.diagonal(upper) < 0, -1.0, 1.0).astype(jnp.float32)
    basis = basis * signs[None, :]
    spectrum = jnp.exp(jax.random.uniform(jax.random.fold_in(shared, 2), (EDGE,), jnp.float32, math.log(0.01), 0.0))

    def single_map(sub_key):
        values = jax.random.normal(sub_key, (full_len, full_len), jnp.float32)
        mixing = jnp.dot(values, values.T, precision=lax.Precision.HIGHEST) / full_len + 0.5 * jnp.eye(full_len, dtype=jnp.float32)
        mixing = 0.5 * (mixing + mixing.T)
        factors = jnp.exp(jax.random.uniform(jax.random.fold_in(sub_key, 3), (4, EDGE), jnp.float32, 0.0, math.log(2.0)))
        roots = jnp.sqrt(spectrum[None, :] * factors).reshape(full_len)
        inner = (roots[:, None] * mixing * roots[None, :]).reshape(4, EDGE, 4, EDGE)
        rotated = jnp.einsum('ia,xaye,je->xiyj', basis, inner, basis, precision=lax.Precision.HIGHEST)
        matrix = rotated.reshape(full_len, full_len)
        return 0.5 * (matrix + matrix.T)
    sub_keys = jax.random.split(key, BOX_COLS * BOX_ROWS)
    maps = lax.map(single_map, sub_keys)
    return maps.reshape(BOX_COLS, BOX_ROWS, full_len, full_len)


def levels(stream_key, shape, cuts, least, high):
    def one(dim, blocks):
        heights = jax.random.uniform(jax.random.fold_in(jax.random.fold_in(stream_key, 6), dim), (blocks,), jnp.float32, least / len(cuts), high / len(cuts))
        return jnp.repeat(jnp.exp(heights), shape[dim] // blocks).reshape((-1,) + (1,) * (len(shape) - dim - 1))

    loudness = one(*cuts[0])
    for cut in cuts[1:]:
        loudness = loudness * one(*cut)
    return loudness


def normal_values(own_key, dims, spread, limit, cuts=(), kind=jnp.bfloat16):
    level = levels(own_key, dims, cuts, -0.22, 0.18) if cuts else 1.0
    entries = jax.random.normal(own_key, dims, jnp.float32) * spread * level
    return jnp.minimum(jnp.maximum(entries, -limit), limit).astype(kind)


def setup_inputs(seed: int = 0) -> dict:
    key_list = jax.random.split(jax.random.key(seed), 3)
    leaf_maps = draw_leaf_maps(jax.random.fold_in(key_list[2], 71), 0)
    edge_data = normal_values(key_list[1], (BOX_COLS, BOX_ROWS, 2 * EDGE, RHS_COUNT), 1.0, 6.0, ((0, 32), (1, 8)), jnp.float32)
    return dict(leaf_maps=leaf_maps, edge_data=edge_data)


def product(left, right):
    return jnp.dot(left.astype(jnp.float32), right.astype(jnp.float32), precision=lax.Precision.HIGHEST, preferred_element_type=jnp.float32)

def solve_definite(matrix, values):
    return jax.scipy.linalg.cho_solve((jnp.linalg.cholesky(matrix), True), values)

def group_solve(inputs):
    blocks, data = inputs
    edge_len = blocks.shape[-1] // 4
    zero_half = jnp.zeros((edge_len, 3 * edge_len), jnp.float32)

    def outside(block, start):
        return jnp.concatenate([block[:, start:start + edge_len], block[:, 2 * edge_len:]], 1)
    zmats = []
    mparts = {}
    rparts = {}
    for row_bit in range(2):
        left_map, right_map = (blocks[0, row_bit], blocks[1, row_bit])
        m_first = left_map[edge_len:2 * edge_len, edge_len:2 * edge_len] + right_map[:edge_len, :edge_len]
        bmat = jnp.concatenate([outside(left_map[edge_len:2 * edge_len], 0), outside(right_map[:edge_len], edge_len)], 1)
        zmat = solve_definite(m_first, bmat)
        zmats.append(zmat)
        y_start = 3 * edge_len - edge_len * row_bit
        prows = [jnp.concatenate([outside(left_map[y_start:y_start + edge_len], 0), zero_half], 1) - product(left_map[y_start:y_start + edge_len, edge_len:2 * edge_len], zmat), jnp.concatenate([zero_half, outside(right_map[y_start:y_start + edge_len], edge_len)], 1) - product(right_map[y_start:y_start + edge_len, :edge_len], zmat)]
        data_left, data_right = (data[0, row_bit], data[1, row_bit])
        for col_bit in range(2):
            half_left = prows[col_bit][:, :3 * edge_len]
            half_right = prows[col_bit][:, 3 * edge_len:]
            y_col = edge_len + edge_len * row_bit
            i_col = 2 * edge_len - edge_len * row_bit
            rparts[col_bit, row_bit] = product(half_left[:, :edge_len], data_left[:edge_len]) + product(half_left[:, y_col:y_col + edge_len], data_left[edge_len:]) + product(half_right[:, :edge_len], data_right[:edge_len]) + product(half_right[:, y_col:y_col + edge_len], data_right[edge_len:])
            mparts[col_bit, row_bit] = jnp.concatenate([half_left[:, i_col:i_col + edge_len], half_right[:, i_col:i_col + edge_len]], 1)
    m_second = jnp.concatenate([mparts[0, 0] + mparts[0, 1], mparts[1, 0] + mparts[1, 1]], 0)
    rhs = jnp.concatenate([rparts[0, 0] + rparts[0, 1], rparts[1, 0] + rparts[1, 1]], 0)
    top = -solve_definite(m_second, rhs)
    top_left, top_right = (top[:edge_len], top[edge_len:])
    potentials = [[None, None], [None, None]]
    fluxes = [[None, None], [None, None]]
    for row_bit in range(2):
        data_left, data_right = (data[0, row_bit], data[1, row_bit])
        if row_bit == 0:
            south_left, north_left = (data_left[edge_len:], top_left)
            south_right, north_right = (data_right[edge_len:], top_right)
        else:
            south_left, north_left = (top_left, data_left[edge_len:])
            south_right, north_right = (top_right, data_right[edge_len:])
        uext = jnp.concatenate([data_left[:edge_len], south_left, north_left, data_right[:edge_len], south_right, north_right], 0)
        middle = -product(zmats[row_bit], uext)
        pot_left = jnp.concatenate([data_left[:edge_len], middle, south_left, north_left], 0)
        pot_right = jnp.concatenate([middle, data_right[:edge_len], south_right, north_right], 0)
        potentials[0][row_bit] = pot_left
        potentials[1][row_bit] = pot_right
        fluxes[0][row_bit] = product(blocks[0, row_bit], pot_left)
        fluxes[1][row_bit] = product(blocks[1, row_bit], pot_right)
    pot_all = jnp.stack([jnp.stack(potentials[0]), jnp.stack(potentials[1])])
    flux_all = jnp.stack([jnp.stack(fluxes[0]), jnp.stack(fluxes[1])])
    return (pot_all, flux_all)

def reference(leaf_maps, edge_data):
    full_len = leaf_maps.shape[-1]
    groups = BOX_COLS // 2 * (BOX_ROWS // 2)
    blocks = leaf_maps.reshape(2, BOX_COLS // 2, 2, BOX_ROWS // 2, full_len, full_len)
    blocks = blocks.transpose(1, 3, 0, 2, 4, 5).reshape(groups, 2, 2, full_len, full_len)
    data = edge_data.reshape(2, BOX_COLS // 2, 2, BOX_ROWS // 2, 2 * EDGE, RHS_COUNT)
    data = data.transpose(1, 3, 0, 2, 4, 5).reshape(groups, 2, 2, 2 * EDGE, RHS_COUNT)
    pot_all, flux_all = lax.map(group_solve, (blocks, data))

    def unfold(values):
        values = values.reshape(BOX_COLS // 2, BOX_ROWS // 2, 2, 2, full_len, RHS_COUNT)
        return values.transpose(2, 0, 3, 1, 4, 5).reshape(BOX_COLS, BOX_ROWS, full_len, RHS_COUNT)
    return (unfold(pot_all), unfold(flux_all))
```

```python
import jax
import jax.numpy as jnp
from jax import lax
from jax.experimental import pallas as pl
from jax.experimental.pallas import tpu as pltpu
from jax.sharding import PartitionSpec as P

F32 = jnp.float32
BF = jnp.bfloat16


def partner(block, axis, stride):
    count = lax.axis_size(axis)
    route = []
    for low in range(count):
        high = low | 1 << stride
        if high != low and high < count:
            route += [(low, high), (high, low)]
    return lax.ppermute(block, axis, route)


def dot(a, b, dims=((1,), (0,))):
    return lax.dot_general(
        a, b, (dims, ((), ())), precision=lax.Precision.HIGHEST, preferred_element_type=F32
    )


def split(v):
    hi = v.astype(BF)
    return hi, (v - hi.astype(F32)).astype(BF)


def dot3(a, b):
    mm = lambda x, y: jnp.dot(x, y, preferred_element_type=F32)
    return mm(a[0], b[0]) + (mm(a[0], b[1]) + mm(a[1], b[0]))


def sub_bcast(v, i):
    return jnp.broadcast_to(v[i : i + 1, :], v.shape)


def lane_bcast(v, j):
    return jnp.broadcast_to(v[:, j : j + 1], v.shape)


def invert_tile(rows):
    lane = lax.broadcasted_iota(jnp.int32, (8, 128), 1)
    subl = lax.broadcasted_iota(jnp.int32, (8, 128), 0)
    rows = list(rows)
    for k in range(len(rows)):
        base = 8 * k
        pan = rows[k]
        inside = (lane >= base) & (lane < base + 8)
        cols = [lane_bcast(pan, base + j) for j in range(8)]
        a = [[sub_bcast(cols[j], i) for j in range(8)] for i in range(8)]
        seeded = jnp.where(inside, jnp.where(lane - base == subl, 1.0, 0.0), pan)
        r = [sub_bcast(seeded, i) for i in range(8)]
        for j in range(8):
            rp = 1.0 / a[j][j]
            r[j] = r[j] * rp
            for q in range(j + 1, 8):
                a[j][q] = a[j][q] * rp
            for i in range(8):
                if i == j:
                    continue
                m = a[i][j]
                for q in range(j + 1, 8):
                    a[i][q] = a[i][q] - m * a[j][q]
                r[i] = r[i] - m * r[j]
        for m in range(len(rows)):
            if m == k:
                continue
            v = rows[m]
            acc = jnp.where(inside, 0.0, v)
            p = [lane_bcast(v, base + j) * r[j] for j in range(8)]
            rows[m] = acc - (((p[0] + p[1]) + (p[2] + p[3])) + ((p[4] + p[5]) + (p[6] + p[7])))
        out = r[0]
        for i in range(1, 8):
            out = jnp.where(subl == i, r[i], out)
        rows[k] = out
    return rows


def invert_into(w):
    n = w.shape[0]

    def body(kb, carry):
        o = pl.multiple_of(kb * 128, 128)
        blk = pl.ds(o, 128)
        rows = invert_tile([w[pl.ds(o + 8 * i, 8), blk] for i in range(16)])
        p = jnp.concatenate(rows, 0)
        rr = dot(p, w[blk, :])
        c = w[:, blk]
        w[:, blk] = jnp.zeros((n, 128), F32)
        w[blk, :] = rr
        w[blk, blk] = p
        rr2 = w[blk, :]
        w[...] = w[...] - dot(c, rr2)
        w[blk, :] = rr2
        return carry

    lax.fori_loop(0, n // 128, body, 0)


def bits():
    col_bit = lax.axis_index("gx") // (lax.axis_size("gx") // 2)
    row_bit = lax.axis_index("gy") // (lax.axis_size("gy") // 2)
    return col_bit, row_bit


def edges(e):
    col_bit, row_bit = bits()
    starts = (e * (1 - col_bit), e * col_bit, 3 * e - e * row_bit, 2 * e + e * row_bit)
    return [pl.multiple_of(s, e) for s in starts]


def vspec():
    return pl.BlockSpec(memory_space=pltpu.VMEM)


def aspec():
    return pl.BlockSpec(memory_space=pl.ANY)


def shape(*dims):
    return jax.ShapeDtypeStruct(dims, F32)


def cost(flops, nbytes):
    return pl.CostEstimate(flops=flops, bytes_accessed=nbytes, transcendentals=0)


def pack_kernel(t_ref, eb_ref, yy_ref, sems):
    e = yy_ref.shape[0]
    inner, _, mid, _ = edges(e)
    copies = [
        pltpu.make_async_copy(
            t_ref.at[pl.ds(inner, e), pl.ds(inner, e)], eb_ref.at[:, pl.ds(0, e)], sems.at[0]
        ),
        pltpu.make_async_copy(
            t_ref.at[pl.ds(inner, e), pl.ds(mid, e)], eb_ref.at[:, pl.ds(e, e)], sems.at[1]
        ),
        pltpu.make_async_copy(t_ref.at[pl.ds(mid, e), pl.ds(mid, e)], yy_ref, sems.at[2]),
    ]
    for c in copies:
        c.start()
    for c in copies:
        c.wait()


def known_kernel(t_ref, g_ref, f_ref, c_ref, d_ref, gh, gl):
    e = g_ref.shape[0] // 2
    step = pl.program_id(0)
    inner, side, mid, outer = edges(e)

    @pl.when(step == 0)
    def _():
        hi, lo = split(g_ref[...])
        gh[...] = hi
        gl[...] = lo

    left = jnp.concatenate([t_ref[:, pl.ds(side, e)], t_ref[:, pl.ds(outer, e)]], 1)
    val = dot3(split(left), (gh[...], gl[...]))
    f_ref[...] = val

    @pl.when(step * e == inner)
    def _():
        c_ref[...] = val

    @pl.when(step * e == mid)
    def _():
        d_ref[...] = val


def first_kernel(eb_ref, sib_ref, yy_ref, x_ref, w_ref, m_ref):
    e = yy_ref.shape[0]
    x_ref[...] = eb_ref[:, :e] + sib_ref[:, :e]
    invert_into(x_ref)
    b_own = eb_ref[:, e:]
    w_ref[:, :e] = dot(x_ref[...], b_own)
    w_ref[:, e:] = dot(x_ref[...], sib_ref[:, e:])
    m_ref[:, :e] = yy_ref[...] - dot(b_own, w_ref[:, :e], ((0,), (0,)))
    m_ref[:, e:] = -dot(b_own, w_ref[:, e:], ((0,), (0,)))


def rhs_kernel(eb_ref, x_ref, c_ref, csib_ref, d_ref, h_ref, ra_ref, rb_ref):
    e = x_ref.shape[0]
    half = ra_ref.shape[1]
    h_ref[...] = dot(x_ref[...], c_ref[...] + csib_ref[...])
    b_own = eb_ref[:, e:]
    ra_ref[...] = d_ref[:, :half] - dot(b_own, h_ref[:, :half], ((0,), (0,)))
    rb_ref[...] = d_ref[:, half:] - dot(b_own, h_ref[:, half:], ((0,), (0,)))


def second_kernel(m_ref, sib_ref, x_ref):
    e = m_ref.shape[0]
    x_ref[:e, :] = m_ref[...]
    x_ref[e:, :e] = sib_ref[:, e:]
    x_ref[e:, e:] = sib_ref[:, :e]
    invert_into(x_ref)


def last_kernel(
    t_ref, g_ref, f_ref, x_ref, w_ref, h_ref, oa_ref, ob_ref, sa_ref, sb_ref, p_ref, q_ref, th, tl
):
    e = w_ref.shape[0]
    step = pl.program_id(0)
    inner, side, mid, outer = edges(e)

    @pl.when(step == 0)
    def _():
        for i in range(4):
            rows = pl.ds(i * e, e)
            left = jnp.concatenate([t_ref[rows, pl.ds(inner, e)], t_ref[rows, pl.ds(mid, e)]], 1)
            hi, lo = split(left)
            th[rows, :] = hi
            tl[rows, :] = lo

    first = step < pl.num_programs(0) // 2
    own = jnp.where(first, oa_ref[...], ob_ref[...])
    sib = jnp.where(first, sa_ref[...], sb_ref[...])
    top = -dot(x_ref[...], jnp.concatenate([own, sib], 0))
    middle = -(h_ref[...] + dot(w_ref[...], top))
    p_ref[pl.ds(inner, e), :] = middle
    p_ref[pl.ds(mid, e), :] = top[:e]
    p_ref[pl.ds(side, e), :] = g_ref[:e, :]
    p_ref[pl.ds(outer, e), :] = g_ref[e:, :]
    right = split(jnp.concatenate([middle, top[:e]], 0))
    q_ref[...] = f_ref[...] + dot3((th[...], tl[...]), right)


def per_device(leaf_maps, edge_data):
    t = leaf_maps[0, 0]
    g = edge_data[0, 0]
    full = t.shape[0]
    cols = g.shape[1]
    e = full // 4
    half = cols // 2
    sx = lax.axis_size("gx").bit_length() - 2
    sz = lax.axis_size("gy").bit_length() - 2

    eb, yy = pl.pallas_call(
        pack_kernel,
        out_shape=(shape(e, 2 * e), shape(e, e)),
        in_specs=[aspec()],
        out_specs=(vspec(), vspec()),
        scratch_shapes=[pltpu.SemaphoreType.DMA((3,))],
        name="pack",
    )(t)
    eb_sib = partner(eb, "gx", sx)
    f0, c, d = pl.pallas_call(
        known_kernel,
        out_shape=(shape(full, cols), shape(e, cols), shape(e, cols)),
        grid=(4,),
        in_specs=[
            pl.BlockSpec((e, full), lambda i: (i, 0)),
            pl.BlockSpec((2 * e, cols), lambda i: (0, 0)),
        ],
        out_specs=(
            pl.BlockSpec((e, cols), lambda i: (i, 0)),
            pl.BlockSpec((e, cols), lambda i: (0, 0)),
            pl.BlockSpec((e, cols), lambda i: (0, 0)),
        ),
        scratch_shapes=[pltpu.VMEM((2 * e, cols), BF), pltpu.VMEM((2 * e, cols), BF)],
        cost_estimate=cost(6 * full * 2 * e * cols, 4 * (full * full + 2 * full * cols)),
        name="known",
    )(t, g)
    c_sib = partner(c, "gx", sx)
    x1, w, m_part = pl.pallas_call(
        first_kernel,
        out_shape=(shape(e, e), shape(e, 2 * e), shape(e, 2 * e)),
        in_specs=[vspec()] * 3,
        out_specs=(vspec(),) * 3,
        cost_estimate=cost(10 * 10**9, 2**21),
        name="first",
    )(eb, eb_sib, yy)
    m_half = m_part + partner(m_part, "gy", sz)
    h, ra, rb = pl.pallas_call(
        rhs_kernel,
        out_shape=(shape(e, cols), shape(e, half), shape(e, half)),
        in_specs=[vspec()] * 5,
        out_specs=(vspec(),) * 3,
        cost_estimate=cost(12 * e * e * cols * 2, 2**22),
        name="rhs",
    )(eb, x1, c, c_sib, d)
    m_sib = partner(m_half, "gx", sx)
    own_a = ra + partner(ra, "gy", sz)
    sib_a = partner(own_a, "gx", sx)
    own_b = rb + partner(rb, "gy", sz)
    sib_b = partner(own_b, "gx", sx)
    x2 = pl.pallas_call(
        second_kernel,
        out_shape=shape(2 * e, 2 * e),
        in_specs=[vspec()] * 2,
        out_specs=vspec(),
        cost_estimate=cost(20 * 10**9, 2**21),
        name="second",
    )(m_half, m_sib)
    lo_map = lambda j: (0, jnp.minimum(j, 1))
    hi_map = lambda j: (0, jnp.maximum(j - 2, 0))
    pot, flux = pl.pallas_call(
        last_kernel,
        out_shape=(shape(full, cols), shape(full, cols)),
        grid=(4,),
        in_specs=[
            pl.BlockSpec((full, full), lambda j: (0, 0)),
            pl.BlockSpec((2 * e, cols // 4), lambda j: (0, j)),
            pl.BlockSpec((full, cols // 4), lambda j: (0, j)),
            pl.BlockSpec((2 * e, 2 * e), lambda j: (0, 0)),
            pl.BlockSpec((e, 2 * e), lambda j: (0, 0)),
            pl.BlockSpec((e, cols // 4), lambda j: (0, j)),
            pl.BlockSpec((e, cols // 4), lo_map),
            pl.BlockSpec((e, cols // 4), hi_map),
            pl.BlockSpec((e, cols // 4), lo_map),
            pl.BlockSpec((e, cols // 4), hi_map),
        ],
        out_specs=(
            pl.BlockSpec((full, cols // 4), lambda j: (0, j)),
            pl.BlockSpec((full, cols // 4), lambda j: (0, j)),
        ),
        scratch_shapes=[pltpu.VMEM((full, 2 * e), BF), pltpu.VMEM((full, 2 * e), BF)],
        cost_estimate=cost(8 * 10**9, 2**24),
        name="last",
    )(t, g, f0, x2, w, h, own_a, own_b, sib_a, sib_b)
    return (pot[None, None], flux[None, None])


def solution(mesh):
    in_specs = (P("gx", "gy", None, None), P("gx", "gy", None, None))
    out_specs = (P("gx", "gy", None, None), P("gx", "gy", None, None))
    return jax.shard_map(
        per_device, mesh=mesh, in_specs=in_specs, out_specs=out_specs, check_vma=False
    )
```

```python
import jax
import jax.numpy as jnp
from jax import lax
from jax.experimental import pallas as pl
from jax.experimental.pallas import tpu as pltpu
from jax.sharding import PartitionSpec as P

F32 = jnp.float32
BF = jnp.bfloat16


def dot(a, b, dims=((1,), (0,))):
    return lax.dot_general(
        a, b, (dims, ((), ())), precision=lax.Precision.HIGHEST, preferred_element_type=F32
    )


def split(v):
    hi = v.astype(BF)
    return hi, (v - hi.astype(F32)).astype(BF)


def dot3(a, b):
    mm = lambda x, y: jnp.dot(x, y, preferred_element_type=F32)
    return mm(a[0], b[0]) + (mm(a[0], b[1]) + mm(a[1], b[0]))


def sub_bcast(v, i):
    return jnp.broadcast_to(v[i : i + 1, :], v.shape)


def lane_bcast(v, j):
    return jnp.broadcast_to(v[:, j : j + 1], v.shape)


def invert_tiles(tiles):
    lane = lax.broadcasted_iota(jnp.int32, (8, 128), 1)
    subl = lax.broadcasted_iota(jnp.int32, (8, 128), 0)
    tiles = [list(t) for t in tiles]
    count = len(tiles[0])
    left = [[] for _ in tiles]
    right = [[] for _ in tiles]
    for k in range(count):
        base = 8 * k
        inside = (lane >= base) & (lane < base + 8)
        seen = lane < base + 8
        eye = jnp.where(lane - base == subl, 1.0, 0.0)
        for ti, rows in enumerate(tiles):
            pan = rows[k]
            cols = [lane_bcast(pan, base + j) for j in range(8)]
            a = [[sub_bcast(cols[j], i) if i >= j else None for j in range(8)] for i in range(8)]
            seeded = jnp.where(inside, eye, pan)
            left[ti].append(jnp.where(seen, seeded, 0.0))
            r = [sub_bcast(seeded, i) for i in range(8)]
            l = [[None] * 8 for _ in range(8)]
            inv = [None] * 8
            for j in range(8):
                if j % 2 == 0:
                    inv[j] = 1.0 / a[j][j]
                    det = a[j][j] * a[j + 1][j + 1] - a[j + 1][j] * a[j + 1][j]
                    inv[j + 1] = a[j][j] * (1.0 / det)
                for i in range(j + 1, 8):
                    l[i][j] = a[i][j] * inv[j]
                for i in range(j + 1, 8):
                    for q in range(j + 1, i + 1):
                        a[i][q] = a[i][q] - l[i][j] * a[q][j]
            for j in range(8):
                for i in range(j + 1, 8):
                    r[i] = r[i] - l[i][j] * r[j]
            for j in range(8):
                r[j] = r[j] * inv[j]
            for j in range(7, 0, -1):
                for i in range(j):
                    r[i] = r[i] - l[j][i] * r[j]
            out = r[0]
            for i in range(1, 8):
                out = jnp.where(subl == i, r[i], out)
            right[ti].append(jnp.where(seen, out, 0.0))
            for m in range(k + 1, count):
                v = rows[m]
                acc = jnp.where(inside, 0.0, v)
                p = [lane_bcast(v, base + j) * r[j] for j in range(8)]
                rows[m] = acc - (((p[0] + p[1]) + (p[2] + p[3])) + ((p[4] + p[5]) + (p[6] + p[7])))
    return [
        dot(jnp.concatenate(x, 0), jnp.concatenate(y, 0), ((0,), (0,)))
        for x, y in zip(left, right)
    ]


def invert_into(ws, hook):
    n = ws[0].shape[0]

    def body(kb, carry):
        hook(kb)
        o = pl.multiple_of(kb * 128, 128)
        blk = pl.ds(o, 128)
        ps = invert_tiles([[w[pl.ds(o + 8 * i, 8), blk] for i in range(16)] for w in ws])
        for w, p in zip(ws, ps):
            rr = dot(p, w[blk, :])
            c = w[:, blk]
            w[:, blk] = jnp.zeros((n, 128), F32)
            w[blk, :] = rr
            w[blk, blk] = p
            rr2 = w[blk, :]
            w[...] = w[...] - dot(c, rr2)
            w[blk, :] = rr2
        return carry

    lax.fori_loop(0, n // 128, body, 0)


def bits():
    col_bit = lax.axis_index("gx") // (lax.axis_size("gx") // 2)
    row_bit = lax.axis_index("gy") // (lax.axis_size("gy") // 2)
    return col_bit, row_bit


def edges(e):
    col_bit, row_bit = bits()
    starts = (e * (1 - col_bit), 3 * e - e * row_bit, e * col_bit, 2 * e + e * row_bit)
    return [pl.multiple_of(s, e) for s in starts]


def peers():
    gx, gy = lax.axis_index("gx"), lax.axis_index("gy")
    nx, ny = lax.axis_size("gx"), lax.axis_size("gy")
    return (lax.rem(gx + nx // 2, nx), gy), (gx, lax.rem(gy + ny // 2, ny))


def vspec():
    return pl.BlockSpec(memory_space=pltpu.VMEM)


def aspec():
    return pl.BlockSpec(memory_space=pl.ANY)


def shape(*dims, dtype=F32):
    return jax.ShapeDtypeStruct(dims, dtype)


def cost(flops, nbytes):
    return pl.CostEstimate(flops=flops, bytes_accessed=nbytes, transcendentals=0)


CHUNKS = 4
MESH = pl.DeviceIdType.MESH


def group_kernel(
    t_ref, g_ref, f_ref, tu_ref, th_ref, tl_ref,
    blk, lft, mid_cols, gv, gh, gl, f0, csib, h, r, rz, rh, rs, x1, x1z, x2, w1, w1z,
    lsem, fsem, xs, xr, zs, zr,
):
    e = x1.shape[0]
    wid = h.shape[2]
    starts = edges(e)
    inner, mid, side, outer = starts
    px, pz = peers()

    def local(src, dst, sem):
        return pltpu.make_async_copy(src, dst, sem)

    rows = lambda s: pl.ds(s, e)
    loads = [
        local(t_ref.at[rows(inner), rows(inner)], blk.at[0, 0], lsem.at[0]),
        local(t_ref.at[rows(inner), rows(mid)], blk.at[0, 1], lsem.at[1]),
        local(t_ref.at[rows(mid), rows(mid)], blk.at[0, 2], lsem.at[2]),
        local(g_ref, gv, lsem.at[3]),
    ]
    for k in range(4):
        for n, s in enumerate((side, outer)):
            loads.append(
                local(t_ref.at[rows(starts[k]), rows(s)], lft.at[k, :, pl.ds(n * e, e)], lsem.at[4 + 2 * k + n])
            )
    for n, s in enumerate((inner, mid)):
        loads.append(local(t_ref.at[:, rows(s)], mid_cols.at[:, pl.ds(n * e, e)], lsem.at[12 + n]))
    for c in loads:
        c.start()

    barrier = pltpu.get_barrier_semaphore()
    for p in (px, pz):
        pl.semaphore_signal(barrier, inc=1, device_id=p, device_id_type=MESH)
    pl.semaphore_wait(barrier, 2)

    def remote(src, dst, ssem, rsem, n, dev):
        return pltpu.make_async_remote_copy(
            src_ref=src, dst_ref=dst, send_sem=ssem.at[n], recv_sem=rsem.at[n],
            device_id=dev, device_id_type=MESH,
        )

    cols = lambda q: pl.ds(q * wid, wid)
    x_blk = [remote(blk.at[0, k], blk.at[1, k], xs, xr, k, px) for k in range(3)]
    z_blk = [remote(blk.at[0, k], blk.at[2, k], zs, zr, k, pz) for k in range(3)]
    x_fwd = [remote(blk.at[2, k], blk.at[3, k], xs, xr, 3 + k, px) for k in range(3)]
    x_c = [remote(f0.at[0, :, cols(q)], csib.at[q], xs, xr, 6 + q, px) for q in range(CHUNKS)]
    x_r = [remote(rh.at[q], rs.at[q], xs, xr, 6 + CHUNKS + q, px) for q in range(CHUNKS)]
    z_r = [remote(r.at[q], rz.at[q], zs, zr, 3 + q, pz) for q in range(CHUNKS)]

    loads[0].wait()
    x_blk[0].start()
    z_blk[0].start()
    loads[1].wait()
    z_blk[1].start()
    loads[2].wait()
    z_blk[2].start()
    loads[3].wait()
    hi, lo = split(gv[...])
    gh[...] = hi
    gl[...] = lo

    def known(k, q):
        sl = pl.ds(pl.multiple_of(q * wid, wid), wid)
        f0[k, :, sl] = dot3(split(lft[k]), (gh[:, sl], gl[:, sl]))

    def save(k):
        return local(f0.at[k], f_ref.at[rows(starts[k]), :], fsem.at[k])

    loads[4].wait()
    loads[5].wait()
    known(0, 0)
    x_c[0].start()
    lax.fori_loop(1, CHUNKS, lambda q, c: (known(0, q), c)[1], 0)
    for c in loads[6:]:
        c.wait()

    def rest(n, carry):
        known(1 + n // CHUNKS, lax.rem(n, CHUNKS))
        return carry

    lax.fori_loop(0, 3 * CHUNKS, rest, 0)
    for k in range(4):
        save(k).start()

    z_blk[0].wait_recv()
    x_fwd[0].start()
    for q in range(1, CHUNKS):
        x_c[q].start()
    x_blk[1].start()
    x_blk[2].start()
    hi, lo = split(mid_cols[...])
    th_ref[...] = hi
    tl_ref[...] = lo
    x_blk[0].wait_recv()
    x1[...] = blk[0, 0] + blk[1, 0]
    x_fwd[0].wait_recv()
    x1z[...] = blk[2, 0] + blk[3, 0]

    def hook_first(kb):
        @pl.when(kb == 1)
        def _():
            z_blk[1].wait_recv()
            x_fwd[1].start()

    invert_into([x1, x1z], hook_first)
    z_blk[2].wait_recv()
    x_fwd[2].start()

    for q in range(CHUNKS):
        x_c[q].wait_recv()
        h[q] = dot(x1[...], f0[0, :, cols(q)] + csib[q])
        r[q] = f0[1, :, cols(q)] - dot(blk[0, 1], h[q], ((0,), (0,)))
        z_r[q].start()

    x_blk[1].wait_recv()
    w1[:, :e] = dot(x1[...], blk[0, 1])
    w1[:, e:] = dot(x1[...], blk[1, 1])
    x_fwd[1].wait_recv()
    w1z[:, :e] = dot(x1z[...], blk[2, 1])
    w1z[:, e:] = dot(x1z[...], blk[3, 1])
    tn = ((0,), (0,))
    cross = dot(blk[0, 1], w1[:, e:], tn) + dot(blk[2, 1], w1z[:, e:], tn)
    x2[:e, e:] = -cross
    x2[e:, :e] = -cross.T
    own = dot(blk[0, 1], w1[:, :e], tn) + dot(blk[2, 1], w1z[:, :e], tn)
    x2[:e, :e] = blk[0, 2] + blk[2, 2] - own
    sib = dot(blk[1, 1], w1[:, e:], tn) + dot(blk[3, 1], w1z[:, e:], tn)
    x_blk[2].wait_recv()
    x_fwd[2].wait_recv()
    x2[e:, e:] = blk[1, 2] + blk[3, 2] - sib

    def forward(q):
        z_r[q].wait_recv()
        rh[q] = r[q] + rz[q]
        x_r[q].start()

    def hook_second(kb):
        for q in range(CHUNKS - 1):

            @pl.when(kb == q + 1)
            def _():
                forward(q)

    invert_into([x2], hook_second)
    forward(CHUNKS - 1)
    for q in range(CHUNKS):
        x_r[q].wait_recv()
        top = -dot(x2[...], jnp.concatenate([rh[q], rs[q]], 0))
        tu_ref[e:, cols(q)] = top[:e]
        tu_ref[:e, cols(q)] = -(h[q] + dot(w1[...], top))

    for c in x_blk + z_blk + x_fwd + x_c + x_r + z_r:
        c.wait_send()
    for k in range(4):
        save(k).wait()


def last_kernel(th_ref, tl_ref, g_ref, f_ref, tu_ref, p_ref, q_ref):
    e = g_ref.shape[0] // 2
    inner, mid, side, outer = edges(e)
    p_ref[pl.ds(inner, e), :] = tu_ref[:e, :]
    p_ref[pl.ds(mid, e), :] = tu_ref[e:, :]
    p_ref[pl.ds(side, e), :] = g_ref[:e, :]
    p_ref[pl.ds(outer, e), :] = g_ref[e:, :]
    q_ref[...] = f_ref[...] + dot3((th_ref[...], tl_ref[...]), split(tu_ref[...]))


def per_device(leaf_maps, edge_data):
    t = leaf_maps[0, 0]
    g = edge_data[0, 0]
    full = t.shape[0]
    cols = g.shape[1]
    e = full // 4
    wid = cols // CHUNKS
    chunk = pltpu.VMEM((CHUNKS, e, wid), F32)
    dma = pltpu.SemaphoreType.DMA
    nx, nz = 6 + 2 * CHUNKS, 3 + CHUNKS

    f0, tu, th, tl = pl.pallas_call(
        group_kernel,
        out_shape=(
            shape(full, cols), shape(2 * e, cols), shape(full, 2 * e, dtype=BF), shape(full, 2 * e, dtype=BF),
        ),
        in_specs=[aspec(), aspec()],
        out_specs=(aspec(), vspec(), vspec(), vspec()),
        scratch_shapes=[
            pltpu.VMEM((4, 3, e, e), F32),
            pltpu.VMEM((4, e, 2 * e), F32),
            pltpu.VMEM((full, 2 * e), F32),
            pltpu.VMEM((2 * e, cols), F32),
            pltpu.VMEM((2 * e, cols), BF),
            pltpu.VMEM((2 * e, cols), BF),
            pltpu.VMEM((4, e, cols), F32),
            chunk, chunk, chunk, chunk, chunk, chunk,
            pltpu.VMEM((e, e), F32),
            pltpu.VMEM((e, e), F32),
            pltpu.VMEM((2 * e, 2 * e), F32),
            pltpu.VMEM((e, 2 * e), F32),
            pltpu.VMEM((e, 2 * e), F32),
            dma((14,)), dma((4,)), dma((nx,)), dma((nx,)), dma((nz,)), dma((nz,)),
        ],
        compiler_params=pltpu.CompilerParams(
            collective_id=0, has_side_effects=True, vmem_limit_bytes=56 * 2**20
        ),
        cost_estimate=cost(20 * 10**9, 2**24),
        name="group",
    )(t, g)
    pot, flux = pl.pallas_call(
        last_kernel,
        out_shape=(shape(full, cols), shape(full, cols)),
        grid=(CHUNKS,),
        in_specs=[
            pl.BlockSpec((full, 2 * e), lambda j: (0, 0)),
            pl.BlockSpec((full, 2 * e), lambda j: (0, 0)),
            pl.BlockSpec((2 * e, wid), lambda j: (0, j)),
            pl.BlockSpec((full, wid), lambda j: (0, j)),
            pl.BlockSpec((2 * e, wid), lambda j: (0, j)),
        ],
        out_specs=(
            pl.BlockSpec((full, wid), lambda j: (0, j)),
            pl.BlockSpec((full, wid), lambda j: (0, j)),
        ),
        cost_estimate=cost(6 * full * 2 * e * cols, 2**24),
        name="last",
    )(th, tl, g, f0, tu)
    return (pot[None, None], flux[None, None])


def solution(mesh):
    in_specs = (P("gx", "gy", None, None), P("gx", "gy", None, None))
    out_specs = (P("gx", "gy", None, None), P("gx", "gy", None, None))
    return jax.shard_map(
        per_device, mesh=mesh, in_specs=in_specs, out_specs=out_specs, check_vma=False
    )
```

```python
import jax
import jax.numpy as jnp
from jax import lax
from jax.experimental import pallas as pl
from jax.experimental.pallas import tpu as pltpu
from jax.sharding import PartitionSpec as P

F32 = jnp.float32
BF = jnp.bfloat16


def dot(a, b, dims=((1,), (0,))):
    return lax.dot_general(
        a, b, (dims, ((), ())), precision=lax.Precision.HIGHEST, preferred_element_type=F32
    )


def split(v):
    hi = v.astype(BF)
    return hi, (v - hi.astype(F32)).astype(BF)


def dot3(a, b):
    mm = lambda x, y: jnp.dot(x, y, preferred_element_type=F32)
    return mm(a[0], b[0]) + (mm(a[0], b[1]) + mm(a[1], b[0]))


def sub_bcast(v, i):
    return jnp.broadcast_to(v[i : i + 1, :], v.shape)


def lane_bcast(v, j):
    return jnp.broadcast_to(v[:, j : j + 1], v.shape)


def invert_tiles(tiles):
    lane = lax.broadcasted_iota(jnp.int32, (8, 128), 1)
    subl = lax.broadcasted_iota(jnp.int32, (8, 128), 0)
    tiles = [list(t) for t in tiles]
    count = len(tiles[0])
    left = [[] for _ in tiles]
    right = [[] for _ in tiles]
    for k in range(count):
        base = 8 * k
        inside = (lane >= base) & (lane < base + 8)
        seen = lane < base + 8
        eye = jnp.where(lane - base == subl, 1.0, 0.0)
        for ti, rows in enumerate(tiles):
            pan = rows[k]
            cols = [lane_bcast(pan, base + j) for j in range(8)]
            a = [[sub_bcast(cols[j], i) if i >= j else None for j in range(8)] for i in range(8)]
            seeded = jnp.where(inside, eye, pan)
            left[ti].append(jnp.where(seen, seeded, 0.0))
            r = [sub_bcast(seeded, i) for i in range(8)]
            l = [[None] * 8 for _ in range(8)]
            inv = [None] * 8
            for j in range(8):
                if j % 2 == 0:
                    inv[j] = 1.0 / a[j][j]
                    det = a[j][j] * a[j + 1][j + 1] - a[j + 1][j] * a[j + 1][j]
                    inv[j + 1] = a[j][j] * (1.0 / det)
                for i in range(j + 1, 8):
                    l[i][j] = a[i][j] * inv[j]
                for i in range(j + 1, 8):
                    for q in range(j + 1, i + 1):
                        a[i][q] = a[i][q] - l[i][j] * a[q][j]
            for j in range(8):
                for i in range(j + 1, 8):
                    r[i] = r[i] - l[i][j] * r[j]
            for j in range(8):
                r[j] = r[j] * inv[j]
            for j in range(7, 0, -1):
                for i in range(j):
                    r[i] = r[i] - l[j][i] * r[j]
            out = r[0]
            for i in range(1, 8):
                out = jnp.where(subl == i, r[i], out)
            right[ti].append(jnp.where(seen, out, 0.0))
            for m in range(k + 1, count):
                v = rows[m]
                acc = jnp.where(inside, 0.0, v)
                p = [lane_bcast(v, base + j) * r[j] for j in range(8)]
                rows[m] = acc - (((p[0] + p[1]) + (p[2] + p[3])) + ((p[4] + p[5]) + (p[6] + p[7])))
    return [
        dot(jnp.concatenate(x, 0), jnp.concatenate(y, 0), ((0,), (0,)))
        for x, y in zip(left, right)
    ]


def invert_into(ws, hook):
    n = ws[0].shape[0]

    def body(kb, carry):
        hook(kb)
        o = pl.multiple_of(kb * 128, 128)
        blk = pl.ds(o, 128)
        ps = invert_tiles([[w[pl.ds(o + 8 * i, 8), blk] for i in range(16)] for w in ws])
        for w, p in zip(ws, ps):
            rr = dot(p, w[blk, :])
            c = w[:, blk]
            w[:, blk] = jnp.zeros((n, 128), F32)
            w[blk, :] = rr
            w[blk, blk] = p
            rr2 = w[blk, :]
            w[...] = w[...] - dot(c, rr2)
            w[blk, :] = rr2
        return carry

    lax.fori_loop(0, n // 128, body, 0)


def bits():
    col_bit = lax.axis_index("gx") // (lax.axis_size("gx") // 2)
    row_bit = lax.axis_index("gy") // (lax.axis_size("gy") // 2)
    return col_bit, row_bit


def edges(e):
    col_bit, row_bit = bits()
    starts = (e * (1 - col_bit), 3 * e - e * row_bit, e * col_bit, 2 * e + e * row_bit)
    return [pl.multiple_of(s, e) for s in starts]


def peers():
    gx, gy = lax.axis_index("gx"), lax.axis_index("gy")
    nx, ny = lax.axis_size("gx"), lax.axis_size("gy")
    return (lax.rem(gx + nx // 2, nx), gy), (gx, lax.rem(gy + ny // 2, ny))


def vspec():
    return pl.BlockSpec(memory_space=pltpu.VMEM)


def aspec():
    return pl.BlockSpec(memory_space=pl.ANY)


def shape(*dims, dtype=F32):
    return jax.ShapeDtypeStruct(dims, dtype)


def cost(flops, nbytes):
    return pl.CostEstimate(flops=flops, bytes_accessed=nbytes, transcendentals=0)


CHUNKS = 4
PIECES = 8
MESH = pl.DeviceIdType.MESH


def group_kernel(
    t_ref, g_ref, f_ref, tu_ref, th_ref, tl_ref,
    blk, lft, mid_cols, gv, gh, gl, f0, csib, h, r, rz, rh, rs, x1, x2, w1,
    mp, mz, mh, ms, x1h, x1l, x2h, x2l, wh, wl, bh, bl,
    lsem, fsem, xs, xr, zs, zr,
):
    e = x1.shape[0]
    half = e // 2
    wid = h.shape[2]
    pie = r.shape[2]
    starts = edges(e)
    inner, mid, side, outer = starts
    px, pz = peers()
    is_left = bits()[0] == 0
    tn = ((0,), (0,))

    rows = lambda s: pl.ds(s, e)
    local = pltpu.make_async_copy
    loads = [
        local(t_ref.at[rows(inner), rows(inner)], blk.at[0, 0], lsem.at[0]),
        local(t_ref.at[rows(inner), rows(mid)], blk.at[0, 1], lsem.at[1]),
        local(t_ref.at[rows(mid), rows(mid)], blk.at[0, 2], lsem.at[2]),
        local(g_ref, gv, lsem.at[3]),
    ]
    for k in range(4):
        for n, s in enumerate((side, outer)):
            loads.append(
                local(t_ref.at[rows(starts[k]), rows(s)], lft.at[k, :, pl.ds(n * e, e)], lsem.at[4 + 2 * k + n])
            )
    for n, s in enumerate((inner, mid)):
        loads.append(local(t_ref.at[:, rows(s)], mid_cols.at[:, pl.ds(n * e, e)], lsem.at[12 + n]))
    for c in loads:
        c.start()

    barrier = pltpu.get_barrier_semaphore()
    for p in (px, pz):
        pl.semaphore_signal(barrier, inc=1, device_id=p, device_id_type=MESH)
    pl.semaphore_wait(barrier, 2)

    def remote(src, dst, ssem, rsem, n, dev):
        return pltpu.make_async_remote_copy(
            src_ref=src, dst_ref=dst, send_sem=ssem.at[n], recv_sem=rsem.at[n],
            device_id=dev, device_id_type=MESH,
        )

    cols = lambda q: pl.ds(pl.multiple_of(q * wid, wid), wid)
    x_blk = [remote(blk.at[0, k], blk.at[1, k], xs, xr, k, px) for k in range(2)]
    x_m = remote(mh, ms, xs, xr, 2, px)
    z_m = remote(mp, mz, zs, zr, 0, pz)
    x_c = lambda q: remote(f0.at[0, :, cols(q)], csib.at[q], xs, xr, 3 + q, px)
    x_r = lambda p: remote(rh.at[p], rs.at[p], xs, xr, 3 + CHUNKS + p, px)
    z_r = lambda p: remote(r.at[p], rz.at[p], zs, zr, 1 + p, pz)

    loads[0].wait()
    x_blk[0].start()
    loads[1].wait()
    x_blk[1].start()
    loads[3].wait()
    hi, lo = split(gv[...])
    gh[...] = hi
    gl[...] = lo

    def known(k, q):
        sl = cols(q)
        f0[k, :, sl] = dot3(split(lft[k]), (gh[:, sl], gl[:, sl]))

    def loop(n, body):
        def step(i, carry):
            body(i)
            return carry

        lax.fori_loop(0, n, step, 0)

    for c in loads[4:8]:
        c.wait()
    loop(CHUNKS, lambda q: known(0, q))
    loop(CHUNKS, lambda q: x_c(q).start())
    loop(CHUNKS, lambda q: known(1, q))
    x_blk[0].wait_recv()
    x1[...] = blk[0, 0] + blk[1, 0]
    invert_into([x1], lambda kb: None)
    x_blk[1].wait_recv()
    loads[2].wait()
    w1[:, :e] = dot(x1[...], blk[0, 1])
    w1[:, e:] = dot(x1[...], blk[1, 1])
    mp[:e, :] = blk[0, 2] - dot(blk[0, 1], w1[:, :e], tn)
    part = jnp.where(is_left, blk[0, 1, :, :half], blk[1, 1, :, half:])
    mp[e:, :] = -dot(part, jnp.where(is_left, w1[:, e:], w1[:, :e]), tn)
    z_m.start()

    def keep(ref_hi, ref_lo, val):
        a, b = split(val)
        ref_hi[...] = a
        ref_lo[...] = b

    keep(x1h, x1l, x1[...])
    keep(wh, wl, w1[...])
    keep(bh, bl, blk[0, 1].T)

    def right(q):
        x_c(q).wait_recv()
        hv = dot3((x1h[...], x1l[...]), split(f0[0, :, cols(q)] + csib[q]))
        h[q] = hv
        rv = f0[1, :, cols(q)] - dot3((bh[...], bl[...]), split(hv))
        for n in range(2):
            r[2 * q + n] = rv[:, n * pie : (n + 1) * pie]
        for n in range(2):
            z_r(2 * q + n).start()

    loop(CHUNKS, right)

    for c in loads[8:]:
        c.wait()
    loop(2 * CHUNKS, lambda n: known(2 + n // CHUNKS, lax.rem(n, CHUNKS)))
    save = [local(f0.at[k], f_ref.at[rows(starts[k]), :], fsem.at[k]) for k in range(4)]
    for c in save:
        c.start()
    keep(th_ref, tl_ref, mid_cols[...])

    z_m.wait_recv()
    mh[...] = mp[...] + mz[...]
    x_m.start()
    x_m.wait_recv()
    x2[:e, :e] = mh[:e, :]
    x2[e:, e:] = ms[:e, :]
    upper = jnp.where(is_left, mh[e:, :], ms[e:, :])
    lower = jnp.where(is_left, ms[e:, :], mh[e:, :])
    cross = jnp.concatenate([upper, lower], 0)
    cross_t = cross.T
    x2[:e, e:] = jnp.where(is_left, cross, cross_t)
    x2[e:, :e] = jnp.where(is_left, cross_t, cross)

    def forward(p):
        z_r(p).wait_recv()
        rh[p] = r[p] + rz[p]
        x_r(p).start()

    def hook(kb):
        @pl.when((kb == 1) | (kb == 2))
        def _():
            forward(2 * kb - 2)
            forward(2 * kb - 1)

        @pl.when(kb == 3)
        def _():
            forward(4)

    invert_into([x2], hook)
    keep(x2h, x2l, x2[...])

    def solve(q):
        @pl.when(q < PIECES - 5)
        def _():
            forward(q + 5)

        x_r(2 * q).wait_recv()
        x_r(2 * q + 1).wait_recv()
        rhs = jnp.concatenate(
            [
                jnp.concatenate([rh[2 * q], rh[2 * q + 1]], 1),
                jnp.concatenate([rs[2 * q], rs[2 * q + 1]], 1),
            ],
            0,
        )
        top = -dot3((x2h[...], x2l[...]), split(rhs))
        tu_ref[e:, cols(q)] = top[:e]
        tu_ref[:e, cols(q)] = -(h[q] + dot3((wh[...], wl[...]), split(top)))

    loop(CHUNKS, solve)

    for c in x_blk + [x_m, z_m]:
        c.wait_send()
    loop(CHUNKS, lambda q: x_c(q).wait_send())

    def sent(p):
        x_r(p).wait_send()
        z_r(p).wait_send()

    loop(PIECES, sent)
    for c in save:
        c.wait()


def last_kernel(th_ref, tl_ref, g_ref, f_ref, tu_ref, p_ref, q_ref):
    e = g_ref.shape[0] // 2
    inner, mid, side, outer = edges(e)
    p_ref[pl.ds(inner, e), :] = tu_ref[:e, :]
    p_ref[pl.ds(mid, e), :] = tu_ref[e:, :]
    p_ref[pl.ds(side, e), :] = g_ref[:e, :]
    p_ref[pl.ds(outer, e), :] = g_ref[e:, :]
    q_ref[...] = f_ref[...] + dot3((th_ref[...], tl_ref[...]), split(tu_ref[...]))


def per_device(leaf_maps, edge_data):
    t = leaf_maps[0, 0]
    g = edge_data[0, 0]
    full = t.shape[0]
    cols = g.shape[1]
    e = full // 4
    wid = cols // CHUNKS
    chunk = pltpu.VMEM((CHUNKS, e, wid), F32)
    piece = pltpu.VMEM((PIECES, e, cols // PIECES), F32)
    half_sum = pltpu.VMEM((e + e // 2, e), F32)
    square = pltpu.VMEM((e, e), BF)
    square2 = pltpu.VMEM((2 * e, 2 * e), BF)
    wide = pltpu.VMEM((e, 2 * e), BF)
    dma = pltpu.SemaphoreType.DMA
    nx, nz = 3 + CHUNKS + PIECES, 1 + PIECES

    f0, tu, th, tl = pl.pallas_call(
        group_kernel,
        out_shape=(
            shape(full, cols), shape(2 * e, cols), shape(full, 2 * e, dtype=BF), shape(full, 2 * e, dtype=BF),
        ),
        in_specs=[aspec(), aspec()],
        out_specs=(aspec(), vspec(), vspec(), vspec()),
        scratch_shapes=[
            pltpu.VMEM((2, 3, e, e), F32),
            pltpu.VMEM((4, e, 2 * e), F32),
            pltpu.VMEM((full, 2 * e), F32),
            pltpu.VMEM((2 * e, cols), F32),
            pltpu.VMEM((2 * e, cols), BF),
            pltpu.VMEM((2 * e, cols), BF),
            pltpu.VMEM((4, e, cols), F32),
            chunk, chunk, piece, piece, piece, piece,
            pltpu.VMEM((e, e), F32),
            pltpu.VMEM((2 * e, 2 * e), F32),
            pltpu.VMEM((e, 2 * e), F32),
            half_sum, half_sum, half_sum, half_sum,
            square, square, square2, square2, wide, wide, square, square,
            dma((14,)), dma((4,)), dma((nx,)), dma((nx,)), dma((nz,)), dma((nz,)),
        ],
        compiler_params=pltpu.CompilerParams(
            collective_id=0, has_side_effects=True, vmem_limit_bytes=56 * 2**20
        ),
        cost_estimate=cost(20 * 10**9, 2**24),
        name="group",
    )(t, g)
    pot, flux = pl.pallas_call(
        last_kernel,
        out_shape=(shape(full, cols), shape(full, cols)),
        grid=(CHUNKS,),
        in_specs=[
            pl.BlockSpec((full, 2 * e), lambda j: (0, 0)),
            pl.BlockSpec((full, 2 * e), lambda j: (0, 0)),
            pl.BlockSpec((2 * e, wid), lambda j: (0, j)),
            pl.BlockSpec((full, wid), lambda j: (0, j)),
            pl.BlockSpec((2 * e, wid), lambda j: (0, j)),
        ],
        out_specs=(
            pl.BlockSpec((full, wid), lambda j: (0, j)),
            pl.BlockSpec((full, wid), lambda j: (0, j)),
        ),
        cost_estimate=cost(6 * full * 2 * e * cols, 2**24),
        name="last",
    )(th, tl, g, f0, tu)
    return (pot[None, None], flux[None, None])


def solution(mesh):
    in_specs = (P("gx", "gy", None, None), P("gx", "gy", None, None))
    out_specs = (P("gx", "gy", None, None), P("gx", "gy", None, None))
    return jax.shard_map(
        per_device, mesh=mesh, in_specs=in_specs, out_specs=out_specs, check_vma=False
    )
```

```python
import jax
import jax.numpy as jnp
from jax import lax
from jax.experimental import pallas as pl
from jax.experimental.pallas import tpu as pltpu
from jax.sharding import PartitionSpec as P

F32 = jnp.float32
BF = jnp.bfloat16


def dot(a, b, dims=((1,), (0,))):
    return lax.dot_general(
        a, b, (dims, ((), ())), precision=lax.Precision.HIGHEST, preferred_element_type=F32
    )


def split(v):
    hi = v.astype(BF)
    return hi, (v - hi.astype(F32)).astype(BF)


def dot3(a, b):
    mm = lambda x, y: jnp.dot(x, y, preferred_element_type=F32)
    return mm(a[0], b[0]) + (mm(a[0], b[1]) + mm(a[1], b[0]))


def sub_bcast(v, i):
    return jnp.broadcast_to(v[i : i + 1, :], v.shape)


def lane_bcast(v, j):
    return jnp.broadcast_to(v[:, j : j + 1], v.shape)


def invert_tiles(tiles):
    lane = lax.broadcasted_iota(jnp.int32, (8, 128), 1)
    subl = lax.broadcasted_iota(jnp.int32, (8, 128), 0)
    tiles = [list(t) for t in tiles]
    count = len(tiles[0])
    left = [[] for _ in tiles]
    right = [[] for _ in tiles]
    for k in range(count):
        base = 8 * k
        inside = (lane >= base) & (lane < base + 8)
        seen = lane < base + 8
        eye = jnp.where(lane - base == subl, 1.0, 0.0)
        for ti, rows in enumerate(tiles):
            pan = rows[k]
            cols = [lane_bcast(pan, base + j) for j in range(8)]
            a = [[sub_bcast(cols[j], i) if i >= j else None for j in range(8)] for i in range(8)]
            seeded = jnp.where(inside, eye, pan)
            left[ti].append(jnp.where(seen, seeded, 0.0))
            r = [sub_bcast(seeded, i) for i in range(8)]
            l = [[None] * 8 for _ in range(8)]
            inv = [None] * 8
            for j in range(8):
                if j % 2 == 0:
                    inv[j] = 1.0 / a[j][j]
                    det = a[j][j] * a[j + 1][j + 1] - a[j + 1][j] * a[j + 1][j]
                    inv[j + 1] = a[j][j] * (1.0 / det)
                for i in range(j + 1, 8):
                    l[i][j] = a[i][j] * inv[j]
                for i in range(j + 1, 8):
                    for q in range(j + 1, i + 1):
                        a[i][q] = a[i][q] - l[i][j] * a[q][j]
            for j in range(8):
                for i in range(j + 1, 8):
                    r[i] = r[i] - l[i][j] * r[j]
            for j in range(8):
                r[j] = r[j] * inv[j]
            for j in range(7, 0, -1):
                for i in range(j):
                    r[i] = r[i] - l[j][i] * r[j]
            out = r[0]
            for i in range(1, 8):
                out = jnp.where(subl == i, r[i], out)
            right[ti].append(jnp.where(seen, out, 0.0))
            for m in range(k + 1, count):
                v = rows[m]
                acc = jnp.where(inside, 0.0, v)
                p = [lane_bcast(v, base + j) * r[j] for j in range(8)]
                rows[m] = acc - (((p[0] + p[1]) + (p[2] + p[3])) + ((p[4] + p[5]) + (p[6] + p[7])))
    return [
        dot(jnp.concatenate(x, 0), jnp.concatenate(y, 0), ((0,), (0,)))
        for x, y in zip(left, right)
    ]


def invert_into(ws, hook, fill):
    n = ws[0].shape[0]

    def body(kb, carry):
        hook(kb)
        o = pl.multiple_of(kb * 128, 128)
        blk = pl.ds(o, 128)
        ps = invert_tiles([[w[pl.ds(o + 8 * i, 8), blk] for i in range(16)] for w in ws])
        fill(kb)
        for w, p in zip(ws, ps):
            rr = dot(p, w[blk, :])
            c = w[:, blk]
            w[:, blk] = jnp.zeros((n, 128), F32)
            w[blk, :] = rr
            w[blk, blk] = p
            rr2 = w[blk, :]
            w[...] = w[...] - dot(c, rr2)
            w[blk, :] = rr2
        return carry

    lax.fori_loop(0, n // 128, body, 0)


def bits():
    col_bit = lax.axis_index("gx") // (lax.axis_size("gx") // 2)
    row_bit = lax.axis_index("gy") // (lax.axis_size("gy") // 2)
    return col_bit, row_bit


def edges(e):
    col_bit, row_bit = bits()
    starts = (e * (1 - col_bit), 3 * e - e * row_bit, e * col_bit, 2 * e + e * row_bit)
    return [pl.multiple_of(s, e) for s in starts]


def peers():
    gx, gy = lax.axis_index("gx"), lax.axis_index("gy")
    nx, ny = lax.axis_size("gx"), lax.axis_size("gy")
    return (lax.rem(gx + nx // 2, nx), gy), (gx, lax.rem(gy + ny // 2, ny))


def vspec():
    return pl.BlockSpec(memory_space=pltpu.VMEM)


def aspec():
    return pl.BlockSpec(memory_space=pl.ANY)


def shape(*dims, dtype=F32):
    return jax.ShapeDtypeStruct(dims, dtype)


def cost(flops, nbytes):
    return pl.CostEstimate(flops=flops, bytes_accessed=nbytes, transcendentals=0)


CHUNKS = 4
PIECES = 8
MESH = pl.DeviceIdType.MESH


def group_kernel(
    t_ref, g_ref, f_ref, tu_ref, th_ref, tl_ref,
    blk, lft, mid_cols, gv, gh, gl, f0, csib, h, r, rz, rh, rs, x1, x2, w1,
    mp, mz, mh, ms, x1h, x1l, x2h, x2l, wh, wl, bh, bl, tuv, thv, tlv,
    lsem, fsem, osem, xs, xr, zs, zr,
):
    e = x1.shape[0]
    half = e // 2
    wid = h.shape[2]
    pie = r.shape[2]
    starts = edges(e)
    inner, mid, side, outer = starts
    px, pz = peers()
    is_left = bits()[0] == 0
    tn = ((0,), (0,))

    rows = lambda s: pl.ds(s, e)
    local = pltpu.make_async_copy
    loads = [
        local(t_ref.at[rows(inner), rows(inner)], blk.at[0, 0], lsem.at[0]),
        local(t_ref.at[rows(inner), rows(mid)], blk.at[0, 1], lsem.at[1]),
        local(t_ref.at[rows(mid), rows(mid)], blk.at[0, 2], lsem.at[2]),
        local(g_ref, gv, lsem.at[3]),
    ]
    for k in range(4):
        for n, s in enumerate((side, outer)):
            loads.append(
                local(t_ref.at[rows(starts[k]), rows(s)], lft.at[k, :, pl.ds(n * e, e)], lsem.at[4 + 2 * k + n])
            )
    for n, s in enumerate((inner, mid)):
        loads.append(local(t_ref.at[:, rows(s)], mid_cols.at[:, pl.ds(n * e, e)], lsem.at[12 + n]))
    for c in loads:
        c.start()

    barrier = pltpu.get_barrier_semaphore()
    for p in (px, pz):
        pl.semaphore_signal(barrier, inc=1, device_id=p, device_id_type=MESH)
    pl.semaphore_wait(barrier, 2)

    def remote(src, dst, ssem, rsem, n, dev):
        return pltpu.make_async_remote_copy(
            src_ref=src, dst_ref=dst, send_sem=ssem.at[n], recv_sem=rsem.at[n],
            device_id=dev, device_id_type=MESH,
        )

    cols = lambda q: pl.ds(pl.multiple_of(q * wid, wid), wid)
    lo, hi = slice(0, half), slice(half, e)
    x_in = [
        remote(blk.at[0, 0, i, j], blk.at[1, 0, i, j], xs, xr, n, px)
        for n, (i, j) in enumerate(
            (pl.ds(p * half, half), pl.ds(q * half, half)) for p, q in ((0, 0), (1, 0), (1, 1))
        )
    ]
    x_b = remote(blk.at[0, 1], blk.at[1, 1], xs, xr, 3, px)
    x_m = remote(mh, ms, xs, xr, 4, px)
    z_m = remote(mp, mz, zs, zr, 0, pz)
    x_c = lambda q: remote(f0.at[0, :, cols(q)], csib.at[q], xs, xr, 5 + q, px)
    x_r = lambda p: remote(rh.at[p], rs.at[p], xs, xr, 5 + CHUNKS + p, px)
    z_r = lambda p: remote(r.at[p], rz.at[p], zs, zr, 1 + p, pz)

    loads[0].wait()
    for c in x_in:
        c.start()
    loads[1].wait()
    x_b.start()

    def keep(ref_hi, ref_lo, val):
        a, b = split(val)
        ref_hi[...] = a
        ref_lo[...] = b

    loads[3].wait()
    keep(gh, gl, gv[...])

    def known(k, q):
        sl = cols(q)
        f0[k, :, sl] = dot3(split(lft[k]), (gh[:, sl], gl[:, sl]))

    def loop(n, body):
        def step(i, carry):
            body(i)
            return carry

        lax.fori_loop(0, n, step, 0)

    for c in loads[4:6]:
        c.wait()
    loop(CHUNKS, lambda q: known(0, q))
    loop(CHUNKS, lambda q: x_c(q).start())

    x_in[0].wait_recv()
    x1[lo, lo] = blk[0, 0, lo, lo] + blk[1, 0, lo, lo]

    def fill_first(kb):
        @pl.when(kb == 0)
        def _():
            x_in[1].wait_recv()
            x_in[2].wait_recv()
            below = blk[0, 0, hi, lo] + blk[1, 0, hi, lo]
            x1[hi, lo] = below
            x1[lo, hi] = below.T
            x1[hi, hi] = blk[0, 0, hi, hi] + blk[1, 0, hi, hi]

    invert_into([x1], lambda kb: None, fill_first)
    x_b.wait_recv()
    loads[2].wait()
    w1[:, :e] = dot(x1[...], blk[0, 1])
    w1[:, e:] = dot(x1[...], blk[1, 1])
    strip = blk[0, 2, :, lo] - dot(blk[0, 1], w1[:, lo], tn)
    mp[0] = strip[lo]
    mp[1] = strip[hi]
    mp[2] = blk[0, 2, hi, hi] - dot(blk[0, 1, :, hi], w1[:, hi], tn)
    part = jnp.where(is_left, blk[0, 1, :, lo], blk[1, 1, :, hi])
    cross = -dot(part, jnp.where(is_left, w1[:, e:], w1[:, :e]), tn)
    mp[3] = cross[:, lo]
    mp[4] = cross[:, hi]
    z_m.start()

    keep(x1h, x1l, x1[...])
    keep(bh, bl, blk[0, 1].T)
    for c in loads[6:8]:
        c.wait()
    loop(CHUNKS, lambda q: known(1, q))

    last = CHUNKS - 1
    parts = [
        local(thv, th_ref, osem.at[0]),
        local(tlv, tl_ref, osem.at[1]),
    ]
    out_t = lambda q: local(tuv.at[:, cols(q)], tu_ref.at[:, cols(q)], osem.at[2 + q])

    def out_f(k, q):
        return local(f0.at[k, :, cols(q)], f_ref.at[rows(starts[k]), cols(q)], fsem.at[k, q])

    def right(q):
        @pl.when(q == 2)
        def _():
            for c in loads[8:]:
                c.wait()
            loop(2 * CHUNKS, lambda n: known(2 + n // CHUNKS, lax.rem(n, CHUNKS)))
            for k in range(4):
                out_f(k, last).start()
            keep(thv, tlv, mid_cols[...])
            for c in parts:
                c.start()
            keep(wh, wl, w1[...])

        x_c(q).wait_recv()
        hv = dot3((x1h[...], x1l[...]), split(f0[0, :, cols(q)] + csib[q]))
        h[q] = hv
        rv = f0[1, :, cols(q)] - dot3((bh[...], bl[...]), split(hv))
        for n in range(2):
            r[2 * q + n] = rv[:, n * pie : (n + 1) * pie]
        for n in range(2):
            z_r(2 * q + n).start()

    loop(CHUNKS, right)

    z_m.wait_recv()
    mh[...] = mp[...] + mz[...]
    x_m.start()
    x2[lo, lo] = mh[0]

    def forward(p):
        z_r(p).wait_recv()
        rh[p] = r[p] + rz[p]
        x_r(p).start()

    def hook(kb):
        @pl.when(kb == 1)
        def _():
            forward(0)

        @pl.when(kb == 2)
        def _():
            forward(1)
            forward(2)

        @pl.when(kb == 3)
        def _():
            forward(3)

    def fill_second(kb):
        @pl.when(kb == 0)
        def _():
            x2[hi, lo] = mh[1]
            x2[lo, hi] = mh[1].T
            x2[hi, hi] = mh[2]
            x_m.wait_recv()
            low, high = slice(e, e + half), slice(e + half, 2 * e)
            x2[low, low] = ms[0]
            x2[high, low] = ms[1]
            x2[low, high] = ms[1].T
            x2[high, high] = ms[2]
            mine = jnp.concatenate([mh[3], mh[4]], 1)
            other = jnp.concatenate([ms[3], ms[4]], 1)
            full = jnp.concatenate(
                [jnp.where(is_left, mine, other), jnp.where(is_left, other, mine)], 0
            )
            full_t = full.T
            x2[:e, e:] = jnp.where(is_left, full, full_t)
            x2[e:, :e] = jnp.where(is_left, full_t, full)

    invert_into([x2], hook, fill_second)
    loop(CHUNKS, lambda q: x_c(q).wait_send())
    forward(4)
    forward(5)
    keep(x2h, x2l, x2[...])

    def solve(q):
        x_r(2 * q).wait_recv()
        x_r(2 * q + 1).wait_recv()
        rhs = jnp.concatenate(
            [
                jnp.concatenate([rh[2 * q], rh[2 * q + 1]], 1),
                jnp.concatenate([rs[2 * q], rs[2 * q + 1]], 1),
            ],
            0,
        )
        top = -dot3((x2h[...], x2l[...]), split(rhs))
        tuv[e:, cols(q)] = top[:e]
        tuv[:e, cols(q)] = -(h[q] + dot3((wh[...], wl[...]), split(top)))
        out_t(q).start()

        @pl.when(q < last)
        def _():
            both = split(tuv[:, cols(q)])
            for k in range(4):
                left = (thv[rows(starts[k]), :], tlv[rows(starts[k]), :])
                f0[k, :, cols(q)] = f0[k, :, cols(q)] + dot3(left, both)
            for k in range(4):
                out_f(k, q).start()

        @pl.when(q < 2)
        def _():
            forward(6 + q)

    loop(CHUNKS, solve)

    for c in x_in + [x_b, x_m, z_m]:
        c.wait_send()

    def sent(p):
        x_r(p).wait_send()
        z_r(p).wait_send()

    loop(PIECES, sent)
    for c in parts:
        c.wait()

    def written(q):
        out_t(q).wait()
        for k in range(4):
            out_f(k, q).wait()

    loop(CHUNKS, written)


def last_kernel(th_ref, tl_ref, g_ref, f_ref, tu_ref, p_ref, q_ref):
    e = g_ref.shape[0] // 2
    inner, mid, side, outer = edges(e)
    p_ref[pl.ds(inner, e), :] = tu_ref[:e, :]
    p_ref[pl.ds(mid, e), :] = tu_ref[e:, :]
    p_ref[pl.ds(side, e), :] = g_ref[:e, :]
    p_ref[pl.ds(outer, e), :] = g_ref[e:, :]
    heavy = pl.program_id(0) == 0

    @pl.when(heavy)
    def _():
        q_ref[...] = f_ref[...] + dot3((th_ref[...], tl_ref[...]), split(tu_ref[...]))

    @pl.when(jnp.logical_not(heavy))
    def _():
        q_ref[...] = f_ref[...]


def per_device(leaf_maps, edge_data):
    t = leaf_maps[0, 0]
    g = edge_data[0, 0]
    full = t.shape[0]
    cols = g.shape[1]
    e = full // 4
    wid = cols // CHUNKS
    chunk = pltpu.VMEM((CHUNKS, e, wid), F32)
    piece = pltpu.VMEM((PIECES, e, cols // PIECES), F32)
    half_sum = pltpu.VMEM((5, e // 2, e // 2), F32)
    square = pltpu.VMEM((e, e), BF)
    square2 = pltpu.VMEM((2 * e, 2 * e), BF)
    wide = pltpu.VMEM((e, 2 * e), BF)
    dma = pltpu.SemaphoreType.DMA
    nx, nz = 5 + CHUNKS + PIECES, 1 + PIECES

    f0, tu, th, tl = pl.pallas_call(
        group_kernel,
        out_shape=(
            shape(full, cols), shape(2 * e, cols), shape(full, 2 * e, dtype=BF), shape(full, 2 * e, dtype=BF),
        ),
        in_specs=[aspec(), aspec()],
        out_specs=(aspec(),) * 4,
        scratch_shapes=[
            pltpu.VMEM((2, 3, e, e), F32),
            pltpu.VMEM((4, e, 2 * e), F32),
            pltpu.VMEM((full, 2 * e), F32),
            pltpu.VMEM((2 * e, cols), F32),
            pltpu.VMEM((2 * e, cols), BF),
            pltpu.VMEM((2 * e, cols), BF),
            pltpu.VMEM((4, e, cols), F32),
            chunk, chunk, piece, piece, piece, piece,
            pltpu.VMEM((e, e), F32),
            pltpu.VMEM((2 * e, 2 * e), F32),
            pltpu.VMEM((e, 2 * e), F32),
            half_sum, half_sum, half_sum, half_sum,
            square, square, square2, square2, wide, wide, square, square,
            pltpu.VMEM((2 * e, cols), F32),
            pltpu.VMEM((full, 2 * e), BF),
            pltpu.VMEM((full, 2 * e), BF),
            dma((14,)), dma((4, CHUNKS)), dma((2 + CHUNKS,)), dma((nx,)), dma((nx,)), dma((nz,)), dma((nz,)),
        ],
        compiler_params=pltpu.CompilerParams(
            collective_id=0, has_side_effects=True, vmem_limit_bytes=56 * 2**20
        ),
        cost_estimate=cost(20 * 10**9, 2**24),
        name="group",
    )(t, g)
    pot, flux = pl.pallas_call(
        last_kernel,
        out_shape=(shape(full, cols), shape(full, cols)),
        grid=(CHUNKS,),
        in_specs=[
            pl.BlockSpec((full, 2 * e), lambda j: (0, 0)),
            pl.BlockSpec((full, 2 * e), lambda j: (0, 0)),
            pl.BlockSpec((2 * e, wid), lambda j: (0, CHUNKS - 1 - j)),
            pl.BlockSpec((full, wid), lambda j: (0, CHUNKS - 1 - j)),
            pl.BlockSpec((2 * e, wid), lambda j: (0, CHUNKS - 1 - j)),
        ],
        out_specs=(
            pl.BlockSpec((full, wid), lambda j: (0, CHUNKS - 1 - j)),
            pl.BlockSpec((full, wid), lambda j: (0, CHUNKS - 1 - j)),
        ),
        cost_estimate=cost(6 * full * 2 * e * cols, 2**24),
        name="last",
    )(th, tl, g, f0, tu)
    return (pot[None, None], flux[None, None])


def solution(mesh):
    in_specs = (P("gx", "gy", None, None), P("gx", "gy", None, None))
    out_specs = (P("gx", "gy", None, None), P("gx", "gy", None, None))
    return jax.shard_map(
        per_device, mesh=mesh, in_specs=in_specs, out_specs=out_specs, check_vma=False
    )
```

```python
import jax
import jax.numpy as jnp
from jax import lax
from jax.experimental import pallas as pl
from jax.experimental.pallas import tpu as pltpu
from jax.sharding import PartitionSpec as P

F32 = jnp.float32
BF = jnp.bfloat16


def dot(a, b, dims=((1,), (0,))):
    return lax.dot_general(
        a, b, (dims, ((), ())), precision=lax.Precision.HIGHEST, preferred_element_type=F32
    )


def split(v):
    hi = v.astype(BF)
    return hi, (v - hi.astype(F32)).astype(BF)


def dot3(a, b):
    mm = lambda x, y: jnp.dot(x, y, preferred_element_type=F32)
    return mm(a[0], b[0]) + (mm(a[0], b[1]) + mm(a[1], b[0]))


def sub_bcast(v, i):
    return jnp.broadcast_to(v[i : i + 1, :], v.shape)


def lane_bcast(v, j):
    return jnp.broadcast_to(v[:, j : j + 1], v.shape)


def invert_tiles(tiles):
    lane = lax.broadcasted_iota(jnp.int32, (8, 128), 1)
    subl = lax.broadcasted_iota(jnp.int32, (8, 128), 0)
    tiles = [list(t) for t in tiles]
    count = len(tiles[0])
    left = [[] for _ in tiles]
    right = [[] for _ in tiles]
    for k in range(count):
        base = 8 * k
        inside = (lane >= base) & (lane < base + 8)
        seen = lane < base + 8
        eye = jnp.where(lane - base == subl, 1.0, 0.0)
        for ti, rows in enumerate(tiles):
            pan = rows[k]
            cols = [lane_bcast(pan, base + j) for j in range(8)]
            a = [[sub_bcast(cols[j], i) if i >= j else None for j in range(8)] for i in range(8)]
            seeded = jnp.where(inside, eye, pan)
            left[ti].append(jnp.where(seen, seeded, 0.0))
            r = [sub_bcast(seeded, i) for i in range(8)]
            l = [[None] * 8 for _ in range(8)]
            inv = [None] * 8
            for j in range(8):
                if j % 2 == 0:
                    inv[j] = 1.0 / a[j][j]
                    det = a[j][j] * a[j + 1][j + 1] - a[j + 1][j] * a[j + 1][j]
                    inv[j + 1] = a[j][j] * (1.0 / det)
                for i in range(j + 1, 8):
                    l[i][j] = a[i][j] * inv[j]
                for i in range(j + 1, 8):
                    for q in range(j + 1, i + 1):
                        a[i][q] = a[i][q] - l[i][j] * a[q][j]
            for j in range(8):
                for i in range(j + 1, 8):
                    r[i] = r[i] - l[i][j] * r[j]
            for j in range(8):
                r[j] = r[j] * inv[j]
            for j in range(7, 0, -1):
                for i in range(j):
                    r[i] = r[i] - l[j][i] * r[j]
            out = r[0]
            for i in range(1, 8):
                out = jnp.where(subl == i, r[i], out)
            right[ti].append(jnp.where(seen, out, 0.0))
            for m in range(k + 1, count):
                v = rows[m]
                acc = jnp.where(inside, 0.0, v)
                p = [lane_bcast(v, base + j) * r[j] for j in range(8)]
                rows[m] = acc - (((p[0] + p[1]) + (p[2] + p[3])) + ((p[4] + p[5]) + (p[6] + p[7])))
    return [
        dot(jnp.concatenate(x, 0), jnp.concatenate(y, 0), ((0,), (0,)))
        for x, y in zip(left, right)
    ]


def invert_into(ws, hook, fill):
    n = ws[0].shape[0]

    def body(kb, carry):
        hook(kb)
        o = pl.multiple_of(kb * 128, 128)
        blk = pl.ds(o, 128)
        ps = invert_tiles([[w[pl.ds(o + 8 * i, 8), blk] for i in range(16)] for w in ws])
        fill(kb)
        for w, p in zip(ws, ps):
            rr = dot(p, w[blk, :])
            c = w[:, blk]
            w[:, blk] = jnp.zeros((n, 128), F32)
            w[blk, :] = rr
            w[blk, blk] = p
            rr2 = w[blk, :]
            w[...] = w[...] - dot(c, rr2)
            w[blk, :] = rr2
        return carry

    lax.fori_loop(0, n // 128, body, 0)


def bits():
    col_bit = lax.axis_index("gx") // (lax.axis_size("gx") // 2)
    row_bit = lax.axis_index("gy") // (lax.axis_size("gy") // 2)
    return col_bit, row_bit


def edges(e):
    col_bit, row_bit = bits()
    starts = (e * (1 - col_bit), 3 * e - e * row_bit, e * col_bit, 2 * e + e * row_bit)
    return [pl.multiple_of(s, e) for s in starts]


def peers():
    gx, gy = lax.axis_index("gx"), lax.axis_index("gy")
    nx, ny = lax.axis_size("gx"), lax.axis_size("gy")
    return (lax.rem(gx + nx // 2, nx), gy), (gx, lax.rem(gy + ny // 2, ny))


def vspec():
    return pl.BlockSpec(memory_space=pltpu.VMEM)


def aspec():
    return pl.BlockSpec(memory_space=pl.ANY)


def hspec():
    return pl.BlockSpec(memory_space=pltpu.HBM)


def shape(*dims, dtype=F32):
    return jax.ShapeDtypeStruct(dims, dtype)


def cost(flops, nbytes):
    return pl.CostEstimate(flops=flops, bytes_accessed=nbytes, transcendentals=0)


CHUNKS = 4
PIECES = 8
MESH = pl.DeviceIdType.MESH


def group_kernel(
    t_ref, g_ref, f_ref, tu_ref, th_ref, tl_ref,
    blk, lft, mid_cols, gv, gh, gl, f0, csib, h, r, rz, rh, rs, x1, x2, w1,
    mp, mz, mh, ms, x1h, x1l, x2h, x2l, wh, wl, bh, bl, tuv, thv, tlv,
    lsem, fsem, osem, xs, xr, zs, zr,
):
    e = x1.shape[0]
    half = e // 2
    wid = h.shape[2]
    pie = r.shape[2]
    starts = edges(e)
    inner, mid, side, outer = starts
    px, pz = peers()
    is_left = bits()[0] == 0
    tn = ((0,), (0,))

    rows = lambda s: pl.ds(s, e)
    local = pltpu.make_async_copy
    loads = [
        local(t_ref.at[rows(inner), rows(inner)], blk.at[0, 0], lsem.at[0]),
        local(t_ref.at[rows(inner), rows(mid)], blk.at[0, 1], lsem.at[1]),
        local(t_ref.at[rows(mid), rows(mid)], blk.at[0, 2], lsem.at[2]),
        local(g_ref, gv, lsem.at[3]),
    ]
    for k in range(4):
        for n, s in enumerate((side, outer)):
            loads.append(
                local(t_ref.at[rows(starts[k]), rows(s)], lft.at[k, :, pl.ds(n * e, e)], lsem.at[4 + 2 * k + n])
            )
    for n, s in enumerate((inner, mid)):
        loads.append(local(t_ref.at[:, rows(s)], mid_cols.at[:, pl.ds(n * e, e)], lsem.at[12 + n]))
    for c in loads:
        c.start()

    barrier = pltpu.get_barrier_semaphore()
    for p in (px, pz):
        pl.semaphore_signal(barrier, inc=1, device_id=p, device_id_type=MESH)
    pl.semaphore_wait(barrier, 2)

    def remote(src, dst, ssem, rsem, n, dev):
        return pltpu.make_async_remote_copy(
            src_ref=src, dst_ref=dst, send_sem=ssem.at[n], recv_sem=rsem.at[n],
            device_id=dev, device_id_type=MESH,
        )

    cols = lambda q: pl.ds(pl.multiple_of(q * wid, wid), wid)
    lo, hi = slice(0, half), slice(half, e)
    x_in = [
        remote(blk.at[0, 0, i, j], blk.at[1, 0, i, j], xs, xr, n, px)
        for n, (i, j) in enumerate(
            (pl.ds(p * half, half), pl.ds(q * half, half)) for p, q in ((0, 0), (1, 0), (1, 1))
        )
    ]
    x_b = remote(blk.at[0, 1], blk.at[1, 1], xs, xr, 3, px)
    x_m = remote(mh, ms, xs, xr, 4, px)
    z_m = [
        remote(mp.at[pl.ds(0, 3)], mz.at[pl.ds(0, 3)], zs, zr, 0, pz),
        remote(mp.at[pl.ds(3, 2)], mz.at[pl.ds(3, 2)], zs, zr, 1 + PIECES, pz),
    ]
    x_c = lambda q: remote(f0.at[0, :, cols(q)], csib.at[q], xs, xr, 5 + q, px)
    x_r = lambda p: remote(rh.at[p], rs.at[p], xs, xr, 5 + CHUNKS + p, px)
    z_r = lambda p: remote(r.at[p], rz.at[p], zs, zr, 1 + p, pz)

    loads[0].wait()
    for c in x_in:
        c.start()
    loads[1].wait()
    x_b.start()

    def keep(ref_hi, ref_lo, val):
        a, b = split(val)
        ref_hi[...] = a
        ref_lo[...] = b

    loads[3].wait()
    keep(gh, gl, gv[...])

    def known(k, q):
        sl = cols(q)
        f0[k, :, sl] = dot3(split(lft[k]), (gh[:, sl], gl[:, sl]))

    def loop(n, body):
        def step(i, carry):
            body(i)
            return carry

        lax.fori_loop(0, n, step, 0)

    for c in loads[4:6]:
        c.wait()
    loop(CHUNKS, lambda q: known(0, q))
    loop(CHUNKS, lambda q: x_c(q).start())

    x_in[0].wait_recv()
    x1[lo, lo] = blk[0, 0, lo, lo] + blk[1, 0, lo, lo]

    def fill_first(kb):
        @pl.when(kb == 0)
        def _():
            x_in[1].wait_recv()
            x_in[2].wait_recv()
            below = blk[0, 0, hi, lo] + blk[1, 0, hi, lo]
            x1[hi, lo] = below
            x1[lo, hi] = below.T
            x1[hi, hi] = blk[0, 0, hi, hi] + blk[1, 0, hi, hi]

    invert_into([x1], lambda kb: None, fill_first)
    loads[2].wait()
    w1[:, :e] = dot(x1[...], blk[0, 1])
    strip = blk[0, 2, :, lo] - dot(blk[0, 1], w1[:, lo], tn)
    mp[0] = strip[lo]
    mp[1] = strip[hi]
    mp[2] = blk[0, 2, hi, hi] - dot(blk[0, 1, :, hi], w1[:, hi], tn)
    z_m[0].start()
    x_b.wait_recv()
    w1[:, e:] = dot(x1[...], blk[1, 1])
    part = jnp.where(is_left, blk[0, 1, :, lo], blk[1, 1, :, hi])
    cross = -dot(part, jnp.where(is_left, w1[:, e:], w1[:, :e]), tn)
    mp[3] = cross[:, lo]
    mp[4] = cross[:, hi]
    z_m[1].start()

    keep(x1h, x1l, x1[...])
    keep(bh, bl, blk[0, 1].T)
    for c in loads[6:8]:
        c.wait()
    loop(CHUNKS, lambda q: known(1, q))

    last = CHUNKS - 1
    parts = [
        local(thv, th_ref, osem.at[0]),
        local(tlv, tl_ref, osem.at[1]),
    ]
    out_t = lambda q: local(tuv.at[:, cols(q)], tu_ref.at[:, cols(q)], osem.at[2 + q])

    def out_f(k, q):
        return local(f0.at[k, :, cols(q)], f_ref.at[rows(starts[k]), cols(q)], fsem.at[k, q])

    def right(q):
        @pl.when(q == 2)
        def _():
            for c in loads[8:]:
                c.wait()
            loop(2 * CHUNKS, lambda n: known(2 + n // CHUNKS, lax.rem(n, CHUNKS)))
            for k in range(4):
                out_f(k, last).start()
            keep(thv, tlv, mid_cols[...])
            for c in parts:
                c.start()
            keep(wh, wl, w1[...])

        x_c(q).wait_recv()
        hv = dot3((x1h[...], x1l[...]), split(f0[0, :, cols(q)] + csib[q]))
        h[q] = hv
        rv = f0[1, :, cols(q)] - dot3((bh[...], bl[...]), split(hv))
        for n in range(2):
            r[2 * q + n] = rv[:, n * pie : (n + 1) * pie]
        for n in range(2):
            z_r(2 * q + n).start()

    loop(CHUNKS, right)

    z_m[0].wait_recv()
    z_m[1].wait_recv()
    mh[...] = mp[...] + mz[...]
    x_m.start()
    x2[lo, lo] = mh[0]

    def forward(p):
        z_r(p).wait_recv()
        rh[p] = r[p] + rz[p]
        x_r(p).start()

    def hook(kb):
        @pl.when(kb == 1)
        def _():
            forward(0)

        @pl.when(kb == 2)
        def _():
            forward(1)
            forward(2)

        @pl.when(kb == 3)
        def _():
            forward(3)

    def fill_second(kb):
        @pl.when(kb == 0)
        def _():
            x2[hi, lo] = mh[1]
            x2[lo, hi] = mh[1].T
            x2[hi, hi] = mh[2]
            x_m.wait_recv()
            low, high = slice(e, e + half), slice(e + half, 2 * e)
            x2[low, low] = ms[0]
            x2[high, low] = ms[1]
            x2[low, high] = ms[1].T
            x2[high, high] = ms[2]
            mine = jnp.concatenate([mh[3], mh[4]], 1)
            other = jnp.concatenate([ms[3], ms[4]], 1)
            full = jnp.concatenate(
                [jnp.where(is_left, mine, other), jnp.where(is_left, other, mine)], 0
            )
            full_t = full.T
            x2[:e, e:] = jnp.where(is_left, full, full_t)
            x2[e:, :e] = jnp.where(is_left, full_t, full)

    invert_into([x2], hook, fill_second)
    loop(CHUNKS, lambda q: x_c(q).wait_send())
    forward(4)
    forward(5)
    keep(x2h, x2l, x2[...])

    def solve(q):
        x_r(2 * q).wait_recv()
        x_r(2 * q + 1).wait_recv()
        rhs = jnp.concatenate(
            [
                jnp.concatenate([rh[2 * q], rh[2 * q + 1]], 1),
                jnp.concatenate([rs[2 * q], rs[2 * q + 1]], 1),
            ],
            0,
        )
        top = -dot3((x2h[...], x2l[...]), split(rhs))
        tuv[e:, cols(q)] = top[:e]
        tuv[:e, cols(q)] = -(h[q] + dot3((wh[...], wl[...]), split(top)))
        out_t(q).start()

        @pl.when(q < last)
        def _():
            both = split(tuv[:, cols(q)])
            for k in range(4):
                left = (thv[rows(starts[k]), :], tlv[rows(starts[k]), :])
                f0[k, :, cols(q)] = f0[k, :, cols(q)] + dot3(left, both)
            for k in range(4):
                out_f(k, q).start()

        @pl.when(q < 2)
        def _():
            forward(6 + q)

    loop(CHUNKS, solve)

    for c in x_in + z_m + [x_b, x_m]:
        c.wait_send()

    def sent(p):
        x_r(p).wait_send()
        z_r(p).wait_send()

    loop(PIECES, sent)
    for c in parts:
        c.wait()

    def written(q):
        out_t(q).wait()
        for k in range(4):
            out_f(k, q).wait()

    loop(CHUNKS, written)


def last_kernel(th_ref, tl_ref, g_ref, f_ref, tu_ref, p_ref, q_ref, thv, tlv, gv, fv, tuv, isem, osem):
    e = g_ref.shape[0] // 2
    cols = g_ref.shape[1]
    done = cols - cols // CHUNKS
    inner, mid, side, outer = edges(e)
    copy = pltpu.make_async_copy
    block = lambda i: pl.ds(i * e, e)
    ready, late = pl.ds(0, done), pl.ds(done, cols - done)
    loads = [
        copy(g_ref, gv, isem.at[0]),
        copy(tu_ref.at[:, late], tuv, isem.at[1]),
        copy(th_ref, thv, isem.at[2]),
        copy(tl_ref, tlv, isem.at[3]),
    ]
    loads += [copy(f_ref.at[block(i), late], fv.at[i], isem.at[4 + i]) for i in range(4)]
    stores = [
        copy(src.at[block(n)], p_ref.at[pl.ds(s, e), :], osem.at[i])
        for i, (src, n, s) in enumerate(
            ((gv, 0, side), (gv, 1, outer), (tu_ref, 0, inner), (tu_ref, 1, mid))
        )
    ]
    stores += [
        copy(f_ref.at[block(i), ready], q_ref.at[block(i), ready], osem.at[4 + i]) for i in range(4)
    ]
    final = [copy(fv.at[i], q_ref.at[block(i), late], osem.at[8 + i]) for i in range(4)]
    for c in loads + stores[2:]:
        c.start()
    loads[0].wait()
    stores[0].start()
    stores[1].start()
    for c in loads[1:4]:
        c.wait()
    both = split(tuv[...])
    for i in range(4):
        loads[4 + i].wait()
        fv[i] = fv[i] + dot3((thv[block(i), :], tlv[block(i), :]), both)
        final[i].start()
    for c in stores + final:
        c.wait()


def per_device(leaf_maps, edge_data):
    t = pltpu.with_memory_space_constraint(leaf_maps[0, 0], pltpu.HBM)
    g = pltpu.with_memory_space_constraint(edge_data[0, 0], pltpu.HBM)
    full = t.shape[0]
    cols = g.shape[1]
    e = full // 4
    wid = cols // CHUNKS
    chunk = pltpu.VMEM((CHUNKS, e, wid), F32)
    piece = pltpu.VMEM((PIECES, e, cols // PIECES), F32)
    half_sum = pltpu.VMEM((5, e // 2, e // 2), F32)
    square = pltpu.VMEM((e, e), BF)
    square2 = pltpu.VMEM((2 * e, 2 * e), BF)
    wide = pltpu.VMEM((e, 2 * e), BF)
    dma = pltpu.SemaphoreType.DMA
    nx, nz = 5 + CHUNKS + PIECES, 2 + PIECES

    f0, tu, th, tl = pl.pallas_call(
        group_kernel,
        out_shape=(
            shape(full, cols), shape(2 * e, cols), shape(full, 2 * e, dtype=BF), shape(full, 2 * e, dtype=BF),
        ),
        in_specs=[hspec(), hspec()],
        out_specs=(aspec(),) * 4,
        scratch_shapes=[
            pltpu.VMEM((2, 3, e, e), F32),
            pltpu.VMEM((4, e, 2 * e), F32),
            pltpu.VMEM((full, 2 * e), F32),
            pltpu.VMEM((2 * e, cols), F32),
            pltpu.VMEM((2 * e, cols), BF),
            pltpu.VMEM((2 * e, cols), BF),
            pltpu.VMEM((4, e, cols), F32),
            chunk, chunk, piece, piece, piece, piece,
            pltpu.VMEM((e, e), F32),
            pltpu.VMEM((2 * e, 2 * e), F32),
            pltpu.VMEM((e, 2 * e), F32),
            half_sum, half_sum, half_sum, half_sum,
            square, square, square2, square2, wide, wide, square, square,
            pltpu.VMEM((2 * e, cols), F32),
            pltpu.VMEM((full, 2 * e), BF),
            pltpu.VMEM((full, 2 * e), BF),
            dma((14,)), dma((4, CHUNKS)), dma((2 + CHUNKS,)), dma((nx,)), dma((nx,)), dma((nz,)), dma((nz,)),
        ],
        compiler_params=pltpu.CompilerParams(
            collective_id=0, has_side_effects=True, vmem_limit_bytes=32 * 2**20
        ),
        cost_estimate=cost(20 * 10**9, 2**24),
        name="group",
    )(t, g)
    pot, flux = pl.pallas_call(
        last_kernel,
        out_shape=(shape(full, cols), shape(full, cols)),
        in_specs=[aspec(), aspec(), hspec(), aspec(), aspec()],
        out_specs=(aspec(), aspec()),
        scratch_shapes=[
            pltpu.VMEM((full, 2 * e), BF),
            pltpu.VMEM((full, 2 * e), BF),
            pltpu.VMEM((2 * e, cols), F32),
            pltpu.VMEM((4, e, wid), F32),
            pltpu.VMEM((2 * e, wid), F32),
            dma((8,)), dma((12,)),
        ],
        compiler_params=pltpu.CompilerParams(vmem_limit_bytes=12 * 2**20),
        cost_estimate=cost(6 * full * 2 * e * cols, 2**24),
        name="last",
    )(th, tl, g, f0, tu)
    return (pot[None, None], flux[None, None])


def solution(mesh):
    in_specs = (P("gx", "gy", None, None), P("gx", "gy", None, None))
    out_specs = (P("gx", "gy", None, None), P("gx", "gy", None, None))
    return jax.shard_map(
        per_device, mesh=mesh, in_specs=in_specs, out_specs=out_specs, check_vma=False
    )
```

```python
import jax
import jax.numpy as jnp
from jax import lax
from jax.experimental import pallas as pl
from jax.experimental.pallas import tpu as pltpu
from jax.sharding import PartitionSpec as P

F32 = jnp.float32
BF = jnp.bfloat16


def dot(a, b, dims=((1,), (0,))):
    return lax.dot_general(
        a, b, (dims, ((), ())), precision=lax.Precision.HIGHEST, preferred_element_type=F32
    )


def split(v):
    hi = v.astype(BF)
    return hi, (v - hi.astype(F32)).astype(BF)


def dot3(a, b):
    mm = lambda x, y: jnp.dot(x, y, preferred_element_type=F32)
    return mm(a[0], b[0]) + (mm(a[0], b[1]) + mm(a[1], b[0]))


def sub_bcast(v, i):
    return jnp.broadcast_to(v[i : i + 1, :], v.shape)


def lane_bcast(v, j):
    return jnp.broadcast_to(v[:, j : j + 1], v.shape)


def invert_tiles(tiles):
    lane = lax.broadcasted_iota(jnp.int32, (8, 128), 1)
    subl = lax.broadcasted_iota(jnp.int32, (8, 128), 0)
    tiles = [list(t) for t in tiles]
    count = len(tiles[0])
    left = [[] for _ in tiles]
    right = [[] for _ in tiles]
    for k in range(count):
        base = 8 * k
        inside = (lane >= base) & (lane < base + 8)
        seen = lane < base + 8
        eye = jnp.where(lane - base == subl, 1.0, 0.0)
        for ti, rows in enumerate(tiles):
            pan = rows[k]
            cols = [lane_bcast(pan, base + j) for j in range(8)]
            a = [[sub_bcast(cols[j], i) if i >= j else None for j in range(8)] for i in range(8)]
            seeded = jnp.where(inside, eye, pan)
            left[ti].append(jnp.where(seen, seeded, 0.0))
            r = [sub_bcast(seeded, i) for i in range(8)]
            l = [[None] * 8 for _ in range(8)]
            inv = [None] * 8
            for j in range(8):
                if j % 2 == 0:
                    inv[j] = 1.0 / a[j][j]
                    det = a[j][j] * a[j + 1][j + 1] - a[j + 1][j] * a[j + 1][j]
                    inv[j + 1] = a[j][j] * (1.0 / det)
                for i in range(j + 1, 8):
                    l[i][j] = a[i][j] * inv[j]
                for i in range(j + 1, 8):
                    for q in range(j + 1, i + 1):
                        a[i][q] = a[i][q] - l[i][j] * a[q][j]
            for j in range(8):
                for i in range(j + 1, 8):
                    r[i] = r[i] - l[i][j] * r[j]
            scaled = [r[j] * inv[j] for j in range(8)]
            if k + 1 < count:
                v = rows[k + 1]
                c = [lane_bcast(v, base + j) for j in range(8)]
                for j in range(8):
                    for i in range(j + 1, 8):
                        c[i] = c[i] - l[i][j] * c[j]
                acc = jnp.where(inside, 0.0, v)
                p = [c[j] * scaled[j] for j in range(8)]
                rows[k + 1] = acc - (((p[0] + p[1]) + (p[2] + p[3])) + ((p[4] + p[5]) + (p[6] + p[7])))
            r = scaled
            for j in range(7, 0, -1):
                for i in range(j):
                    r[i] = r[i] - l[j][i] * r[j]
            out = r[0]
            for i in range(1, 8):
                out = jnp.where(subl == i, r[i], out)
            right[ti].append(jnp.where(seen, out, 0.0))
            rest = {m: rows[m] for m in range(k + 2, count)}
            accs = {m: jnp.where(inside, 0.0, v) for m, v in rest.items()}
            for j in range(8):
                for m, v in rest.items():
                    accs[m] = accs[m] - lane_bcast(v, base + j) * r[j]
            for m, v in accs.items():
                rows[m] = v
    return [
        dot(jnp.concatenate(x, 0), jnp.concatenate(y, 0), ((0,), (0,)))
        for x, y in zip(left, right)
    ]


def invert_into(ws, hook, fill):
    n = ws[0].shape[0]

    def body(kb, carry):
        hook(kb)
        o = pl.multiple_of(kb * 128, 128)
        blk = pl.ds(o, 128)
        ps = invert_tiles([[w[pl.ds(o + 8 * i, 8), blk] for i in range(16)] for w in ws])
        fill(kb)
        for w, p in zip(ws, ps):
            rr = dot(p, w[blk, :])
            c = w[:, blk]
            w[:, blk] = jnp.zeros((n, 128), F32)
            w[blk, :] = rr
            w[blk, blk] = p
            rr2 = w[blk, :]
            w[...] = w[...] - dot(c, rr2)
            w[blk, :] = rr2
        return carry

    lax.fori_loop(0, n // 128, body, 0)


def bits():
    col_bit = lax.axis_index("gx") // (lax.axis_size("gx") // 2)
    row_bit = lax.axis_index("gy") // (lax.axis_size("gy") // 2)
    return col_bit, row_bit


def edges(e):
    col_bit, row_bit = bits()
    starts = (e * (1 - col_bit), 3 * e - e * row_bit, e * col_bit, 2 * e + e * row_bit)
    return [pl.multiple_of(s, e) for s in starts]


def peers():
    gx, gy = lax.axis_index("gx"), lax.axis_index("gy")
    nx, ny = lax.axis_size("gx"), lax.axis_size("gy")
    return (lax.rem(gx + nx // 2, nx), gy), (gx, lax.rem(gy + ny // 2, ny))


def vspec():
    return pl.BlockSpec(memory_space=pltpu.VMEM)


def aspec():
    return pl.BlockSpec(memory_space=pl.ANY)


def hspec():
    return pl.BlockSpec(memory_space=pltpu.HBM)


def shape(*dims, dtype=F32):
    return jax.ShapeDtypeStruct(dims, dtype)


def cost(flops, nbytes):
    return pl.CostEstimate(flops=flops, bytes_accessed=nbytes, transcendentals=0)


CHUNKS = 4
PIECES = 8
MESH = pl.DeviceIdType.MESH


def group_kernel(
    t_ref, g_ref, f_ref, tu_ref, th_ref, tl_ref,
    blk, lft, mid_cols, gv, gh, gl, f0, csib, h, r, rz, rh, rs, x1, x2, w1,
    mp, mz, mh, ms, x1h, x1l, x2h, x2l, wh, wl, bh, bl, tuv, thv, tlv,
    lsem, fsem, osem, xs, xr, zs, zr,
):
    e = x1.shape[0]
    half = e // 2
    wid = h.shape[2]
    pie = r.shape[2]
    starts = edges(e)
    inner, mid, side, outer = starts
    px, pz = peers()
    is_left = bits()[0] == 0
    tn = ((0,), (0,))

    rows = lambda s: pl.ds(s, e)
    local = pltpu.make_async_copy
    loads = [
        local(t_ref.at[rows(inner), rows(inner)], blk.at[0, 0], lsem.at[0]),
        local(t_ref.at[rows(inner), rows(mid)], blk.at[0, 1], lsem.at[1]),
        local(t_ref.at[rows(mid), rows(mid)], blk.at[0, 2], lsem.at[2]),
        local(g_ref, gv, lsem.at[3]),
    ]
    for k in range(4):
        for n, s in enumerate((side, outer)):
            loads.append(
                local(t_ref.at[rows(starts[k]), rows(s)], lft.at[k, :, pl.ds(n * e, e)], lsem.at[4 + 2 * k + n])
            )
    for n, s in enumerate((inner, mid)):
        loads.append(local(t_ref.at[:, rows(s)], mid_cols.at[:, pl.ds(n * e, e)], lsem.at[12 + n]))
    for c in loads:
        c.start()

    barrier = pltpu.get_barrier_semaphore()
    for p in (px, pz):
        pl.semaphore_signal(barrier, inc=1, device_id=p, device_id_type=MESH)
    pl.semaphore_wait(barrier, 2)

    def remote(src, dst, ssem, rsem, n, dev):
        return pltpu.make_async_remote_copy(
            src_ref=src, dst_ref=dst, send_sem=ssem.at[n], recv_sem=rsem.at[n],
            device_id=dev, device_id_type=MESH,
        )

    cols = lambda q: pl.ds(pl.multiple_of(q * wid, wid), wid)
    lo, hi = slice(0, half), slice(half, e)
    x_in = [
        remote(blk.at[0, 0, i, j], blk.at[1, 0, i, j], xs, xr, n, px)
        for n, (i, j) in enumerate(
            (pl.ds(p * half, half), pl.ds(q * half, half)) for p, q in ((0, 0), (1, 0), (1, 1))
        )
    ]
    x_b = remote(blk.at[0, 1], blk.at[1, 1], xs, xr, 3, px)
    x_m = remote(mh, ms, xs, xr, 4, px)
    z_m = [
        remote(mp.at[pl.ds(0, 3)], mz.at[pl.ds(0, 3)], zs, zr, 0, pz),
        remote(mp.at[pl.ds(3, 2)], mz.at[pl.ds(3, 2)], zs, zr, 1 + PIECES, pz),
    ]
    x_c = lambda q: remote(f0.at[0, :, cols(q)], csib.at[q], xs, xr, 5 + q, px)
    x_r = lambda p: remote(rh.at[p], rs.at[p], xs, xr, 5 + CHUNKS + p, px)
    z_r = lambda p: remote(r.at[p], rz.at[p], zs, zr, 1 + p, pz)

    loads[0].wait()
    for c in x_in:
        c.start()
    loads[1].wait()
    x_b.start()

    def keep(ref_hi, ref_lo, val):
        a, b = split(val)
        ref_hi[...] = a
        ref_lo[...] = b

    loads[3].wait()
    keep(gh, gl, gv[...])

    def known(k, q):
        sl = cols(q)
        f0[k, :, sl] = dot3(split(lft[k]), (gh[:, sl], gl[:, sl]))

    def loop(n, body):
        def step(i, carry):
            body(i)
            return carry

        lax.fori_loop(0, n, step, 0)

    for c in loads[4:6]:
        c.wait()
    loop(CHUNKS, lambda q: known(0, q))
    loop(CHUNKS, lambda q: x_c(q).start())

    x_in[0].wait_recv()
    x1[lo, lo] = blk[0, 0, lo, lo] + blk[1, 0, lo, lo]

    def fill_first(kb):
        @pl.when(kb == 0)
        def _():
            x_in[1].wait_recv()
            x_in[2].wait_recv()
            below = blk[0, 0, hi, lo] + blk[1, 0, hi, lo]
            x1[hi, lo] = below
            x1[lo, hi] = below.T
            x1[hi, hi] = blk[0, 0, hi, hi] + blk[1, 0, hi, hi]

    invert_into([x1], lambda kb: None, fill_first)
    loads[2].wait()
    keep(x1h, x1l, x1[...])
    keep(bh, bl, blk[0, 1].T)
    w1[:, :e] = dot3((x1h[...], x1l[...]), split(blk[0, 1]))
    ws = split(w1[:, :e])
    strip = blk[0, 2] - dot3((bh[...], bl[...]), ws)
    mp[0] = strip[lo, lo]
    mp[1] = strip[hi, lo]
    mp[2] = strip[hi, hi]
    z_m[0].start()
    x_b.wait_recv()
    w1[:, e:] = dot3((x1h[...], x1l[...]), split(blk[1, 1]))
    part = jnp.where(is_left, blk[0, 1, :, lo], blk[1, 1, :, hi])
    cross = -dot(part, jnp.where(is_left, w1[:, e:], w1[:, :e]), tn)
    mp[3] = cross[:, lo]
    mp[4] = cross[:, hi]
    z_m[1].start()

    for c in loads[6:8]:
        c.wait()
    loop(CHUNKS, lambda q: known(1, q))

    last = CHUNKS - 1
    parts = [
        local(thv, th_ref, osem.at[0]),
        local(tlv, tl_ref, osem.at[1]),
    ]
    out_t = lambda q: local(tuv.at[:, cols(q)], tu_ref.at[:, cols(q)], osem.at[2 + q])

    def out_f(k, q):
        return local(f0.at[k, :, cols(q)], f_ref.at[rows(starts[k]), cols(q)], fsem.at[k, q])

    def right(q):
        @pl.when(q == 2)
        def _():
            for c in loads[8:]:
                c.wait()
            loop(2 * CHUNKS, lambda n: known(2 + n // CHUNKS, lax.rem(n, CHUNKS)))
            for k in range(4):
                out_f(k, last).start()
            keep(thv, tlv, mid_cols[...])
            for c in parts:
                c.start()
            keep(wh, wl, w1[...])

        x_c(q).wait_recv()
        hv = dot3((x1h[...], x1l[...]), split(f0[0, :, cols(q)] + csib[q]))
        h[q] = hv
        rv = f0[1, :, cols(q)] - dot3((bh[...], bl[...]), split(hv))
        for n in range(2):
            r[2 * q + n] = rv[:, n * pie : (n + 1) * pie]
        for n in range(2):
            z_r(2 * q + n).start()

    loop(CHUNKS, right)

    z_m[0].wait_recv()
    z_m[1].wait_recv()
    mh[...] = mp[...] + mz[...]
    x_m.start()
    x2[lo, lo] = mh[0]

    def forward(p):
        z_r(p).wait_recv()
        rh[p] = r[p] + rz[p]
        x_r(p).start()

    def hook(kb):
        @pl.when(kb == 1)
        def _():
            forward(0)

        @pl.when(kb == 2)
        def _():
            forward(1)
            forward(2)

        @pl.when(kb == 3)
        def _():
            forward(3)

    def fill_second(kb):
        @pl.when(kb == 0)
        def _():
            x2[hi, lo] = mh[1]
            x2[lo, hi] = mh[1].T
            x2[hi, hi] = mh[2]
            x_m.wait_recv()
            low, high = slice(e, e + half), slice(e + half, 2 * e)
            x2[low, low] = ms[0]
            x2[high, low] = ms[1]
            x2[low, high] = ms[1].T
            x2[high, high] = ms[2]
            mine = jnp.concatenate([mh[3], mh[4]], 1)
            other = jnp.concatenate([ms[3], ms[4]], 1)
            full = jnp.concatenate(
                [jnp.where(is_left, mine, other), jnp.where(is_left, other, mine)], 0
            )
            full_t = full.T
            x2[:e, e:] = jnp.where(is_left, full, full_t)
            x2[e:, :e] = jnp.where(is_left, full_t, full)

    invert_into([x2], hook, fill_second)
    loop(CHUNKS, lambda q: x_c(q).wait_send())
    forward(4)
    forward(5)
    keep(x2h, x2l, x2[...])

    def solve(q):
        x_r(2 * q).wait_recv()
        x_r(2 * q + 1).wait_recv()
        rhs = jnp.concatenate(
            [
                jnp.concatenate([rh[2 * q], rh[2 * q + 1]], 1),
                jnp.concatenate([rs[2 * q], rs[2 * q + 1]], 1),
            ],
            0,
        )
        top = -dot3((x2h[...], x2l[...]), split(rhs))
        tuv[e:, cols(q)] = top[:e]
        tuv[:e, cols(q)] = -(h[q] + dot3((wh[...], wl[...]), split(top)))
        out_t(q).start()

        @pl.when(q < last)
        def _():
            both = split(tuv[:, cols(q)])
            for k in range(4):
                left = (thv[rows(starts[k]), :], tlv[rows(starts[k]), :])
                f0[k, :, cols(q)] = f0[k, :, cols(q)] + dot3(left, both)
            for k in range(4):
                out_f(k, q).start()

        @pl.when(q < 2)
        def _():
            forward(6 + q)

    loop(CHUNKS, solve)

    for c in x_in + z_m + [x_b, x_m]:
        c.wait_send()

    def sent(p):
        x_r(p).wait_send()
        z_r(p).wait_send()

    loop(PIECES, sent)
    for c in parts:
        c.wait()

    def written(q):
        out_t(q).wait()
        for k in range(4):
            out_f(k, q).wait()

    loop(CHUNKS, written)


def last_kernel(th_ref, tl_ref, g_ref, f_ref, tu_ref, p_ref, q_ref, thv, tlv, gv, fv, tuv, isem, osem):
    e = g_ref.shape[0] // 2
    cols = g_ref.shape[1]
    done = cols - cols // CHUNKS
    inner, mid, side, outer = edges(e)
    copy = pltpu.make_async_copy
    block = lambda i: pl.ds(i * e, e)
    ready, late = pl.ds(0, done), pl.ds(done, cols - done)
    loads = [
        copy(g_ref, gv, isem.at[0]),
        copy(tu_ref.at[:, late], tuv, isem.at[1]),
        copy(th_ref, thv, isem.at[2]),
        copy(tl_ref, tlv, isem.at[3]),
    ]
    loads += [copy(f_ref.at[block(i), late], fv.at[i], isem.at[4 + i]) for i in range(4)]
    stores = [
        copy(src.at[block(n)], p_ref.at[pl.ds(s, e), :], osem.at[i])
        for i, (src, n, s) in enumerate(
            ((gv, 0, side), (gv, 1, outer), (tu_ref, 0, inner), (tu_ref, 1, mid))
        )
    ]
    stores += [
        copy(f_ref.at[block(i), ready], q_ref.at[block(i), ready], osem.at[4 + i]) for i in range(4)
    ]
    final = [copy(fv.at[i], q_ref.at[block(i), late], osem.at[8 + i]) for i in range(4)]
    for c in loads + stores[2:]:
        c.start()
    loads[0].wait()
    stores[0].start()
    stores[1].start()
    for c in loads[1:4]:
        c.wait()
    both = split(tuv[...])
    for i in range(4):
        loads[4 + i].wait()
        fv[i] = fv[i] + dot3((thv[block(i), :], tlv[block(i), :]), both)
        final[i].start()
    for c in stores + final:
        c.wait()


def per_device(leaf_maps, edge_data):
    t = pltpu.with_memory_space_constraint(leaf_maps[0, 0], pltpu.HBM)
    g = pltpu.with_memory_space_constraint(edge_data[0, 0], pltpu.HBM)
    full = t.shape[0]
    cols = g.shape[1]
    e = full // 4
    wid = cols // CHUNKS
    chunk = pltpu.VMEM((CHUNKS, e, wid), F32)
    piece = pltpu.VMEM((PIECES, e, cols // PIECES), F32)
    half_sum = pltpu.VMEM((5, e // 2, e // 2), F32)
    square = pltpu.VMEM((e, e), BF)
    square2 = pltpu.VMEM((2 * e, 2 * e), BF)
    wide = pltpu.VMEM((e, 2 * e), BF)
    dma = pltpu.SemaphoreType.DMA
    nx, nz = 5 + CHUNKS + PIECES, 2 + PIECES

    f0, tu, th, tl = pl.pallas_call(
        group_kernel,
        out_shape=(
            shape(full, cols), shape(2 * e, cols), shape(full, 2 * e, dtype=BF), shape(full, 2 * e, dtype=BF),
        ),
        in_specs=[hspec(), hspec()],
        out_specs=(aspec(),) * 4,
        scratch_shapes=[
            pltpu.VMEM((2, 3, e, e), F32),
            pltpu.VMEM((4, e, 2 * e), F32),
            pltpu.VMEM((full, 2 * e), F32),
            pltpu.VMEM((2 * e, cols), F32),
            pltpu.VMEM((2 * e, cols), BF),
            pltpu.VMEM((2 * e, cols), BF),
            pltpu.VMEM((4, e, cols), F32),
            chunk, chunk, piece, piece, piece, piece,
            pltpu.VMEM((e, e), F32),
            pltpu.VMEM((2 * e, 2 * e), F32),
            pltpu.VMEM((e, 2 * e), F32),
            half_sum, half_sum, half_sum, half_sum,
            square, square, square2, square2, wide, wide, square, square,
            pltpu.VMEM((2 * e, cols), F32),
            pltpu.VMEM((full, 2 * e), BF),
            pltpu.VMEM((full, 2 * e), BF),
            dma((14,)), dma((4, CHUNKS)), dma((2 + CHUNKS,)), dma((nx,)), dma((nx,)), dma((nz,)), dma((nz,)),
        ],
        compiler_params=pltpu.CompilerParams(
            collective_id=0, has_side_effects=True, vmem_limit_bytes=32 * 2**20
        ),
        cost_estimate=cost(20 * 10**9, 2**24),
        name="group",
    )(t, g)
    pot, flux = pl.pallas_call(
        last_kernel,
        out_shape=(shape(full, cols), shape(full, cols)),
        in_specs=[aspec(), aspec(), hspec(), aspec(), aspec()],
        out_specs=(aspec(), aspec()),
        scratch_shapes=[
            pltpu.VMEM((full, 2 * e), BF),
            pltpu.VMEM((full, 2 * e), BF),
            pltpu.VMEM((2 * e, cols), F32),
            pltpu.VMEM((4, e, wid), F32),
            pltpu.VMEM((2 * e, wid), F32),
            dma((8,)), dma((12,)),
        ],
        compiler_params=pltpu.CompilerParams(vmem_limit_bytes=12 * 2**20),
        cost_estimate=cost(6 * full * 2 * e * cols, 2**24),
        name="last",
    )(th, tl, g, f0, tu)
    return (pot[None, None], flux[None, None])


def solution(mesh):
    in_specs = (P("gx", "gy", None, None), P("gx", "gy", None, None))
    out_specs = (P("gx", "gy", None, None), P("gx", "gy", None, None))
    return jax.shard_map(
        per_device, mesh=mesh, in_specs=in_specs, out_specs=out_specs, check_vma=False
    )
```
